256 devices in a mesh: gx: 8 (over x_hi, y), gy: 16 (over z, x_lo), af: 2 (over core).
Axes of the slice: x: 4 (x_hi: 2, x_lo: 2; x = x_hi * 2 + x_lo), y: 4, z: 8, core: 2. Of those that a mesh axis runs over, the one named last changes fastest.
Arguments:
- model: float32 [256, 512, 128], P('gx', 'gy'), may hold values from 0.5 to 2
- freq_sq: float32 [4], P('af'), may hold values from 0.5 to 3
- source: float32 [4, 2, 256, 512, 128], P('af', None, 'gx', 'gy'), may hold values from -20 to 20
- observed: float32 [4, 2, 256, 512], P('af', None, 'gx', 'gy'), may hold values from -6 to 6
- receiver_depth: int32 [256, 512], P('gx', 'gy'), may hold values from 0 to 3
Outputs:
- wavefield: float32 [4, 2, 256, 512, 128], P('af', None, 'gx', 'gy')
- gradient: float32 [256, 512, 128], P('gx', 'gy')
The draws below stay inside these ranges and needn't reach their ends.
Inputs may be any that keep to these rules, and one draw needn't show every extreme that they name: `receiver_depth`: every surface column holds one receiver, at the given depth index.
All inputs are finite; a program needn't handle non-finite values.
Results may differ from the reference program's by a relative error of at most 0.00012.
Values sent between devices are 32-bit elements; how exact they have to be, the bound alone decides.
A program may use at most 64 MiB of HBM per device.

```python
import math
import jax
import jax.numpy as jnp

CZ = 128
ITERS = 2
RDEPTH = 4
NF = 4
NX = 256
NY = 512


def draw_source(key, part):
    first, second = jax.random.split(jax.random.fold_in(key, 11), 2)
    shape = (NF, 2, NX, NY, CZ)
    column = jnp.exp(jax.random.uniform(second, (NX, NY, 1), jnp.float32, -0.7, 0.7))
    base = jnp.clip(jax.random.normal(first, shape, jnp.float32), -3.0, 3.0)
    ramp = 1.0 + 2.0 * jnp.arange(NX, dtype=jnp.float32)[:, None, None] / max(NX - 1, 1)
    return (base * ramp * column).astype(jnp.float32)


def set_ends(entries, own_key, smallest, top_value):
    index_at = [jax.random.randint(jax.random.fold_in(own_key, axis), (), 0, length) for axis, length in enumerate(entries.shape)]
    longest = entries.shape.index(max(entries.shape))
    beside = index_at[:longest] + [(index_at[longest] + 1) % entries.shape[longest]] + index_at[longest + 1:]
    return entries.at[tuple(index_at)].set(smallest).at[tuple(beside)].set(top_value)


def steps_of(key, extent, pieces, least, largest):
    gain, own = 1.0, jax.random.fold_in(key, 6)
    for dim, shards_of in pieces:
        heights = jnp.exp(jax.random.uniform(jax.random.fold_in(own, dim), (shards_of,), jnp.float32, least / len(pieces), largest / len(pieces)))
        gain = gain * jnp.repeat(heights, extent[dim] // shards_of).reshape([-1 if axis == dim else 1 for axis in range(len(extent))])
    return gain


def noise(own_key, shape, scale, bound, cuts=(), kind=jnp.bfloat16):
    factor_of = steps_of(own_key, shape, cuts, -0.22, 0.18) if cuts else 1.0
    values = jax.random.normal(own_key, shape, jnp.float32) * scale * factor_of
    return jnp.minimum(jnp.maximum(values, -bound), bound).astype(kind)


def setup_inputs(seed: int = 0) -> dict:
    keys = jax.random.split(jax.random.key(seed), 6)
    return {
        "model": jnp.clip(jnp.exp(math.log(2.0) - 1.3862944 * jax.random.uniform(keys[0], (NX, NY, CZ), jnp.float32) ** steps_of(keys[0], (NX, NY, CZ), ((0, 8), (1, 16)), -0.2, 0.2)), 0.5, 2.0),
        "freq_sq": jnp.clip(jnp.exp(math.log(3.0) - 1.7917595 * jax.random.uniform(keys[1], (NF,), jnp.float32) ** steps_of(keys[1], (NF,), ((0, 2),), -0.2, 0.2)), 0.5, 3.0),
        "source": draw_source(jax.random.fold_in(keys[5], 71), 0),
        "observed": noise(keys[3], (NF, 2, NX, NY), 1.0, 6.0, ((0, 2), (2, 8), (3, 16)), jnp.float32),
        "receiver_depth": set_ends(jax.random.randint(keys[4], (NX, NY), 0, RDEPTH), jax.random.fold_in(keys[4], 1), 0, RDEPTH - 1).astype(jnp.int32),
    }


attenuation = 0.2
penalty = 4.0


def neighbours(field):
    padded = jnp.pad(field, ((0, 0), (1, 1), (1, 1), (1, 1)))
    total = padded[:, 2:, 1:-1, 1:-1] + padded[:, :-2, 1:-1, 1:-1]
    total = total + padded[:, 1:-1, 2:, 1:-1] + padded[:, 1:-1, :-2, 1:-1]
    total = total + padded[:, 1:-1, 1:-1, 2:] + padded[:, 1:-1, 1:-1, :-2]
    return total


def apply_coef(coef_real, coef_imag, field, sign):
    real_part = coef_real * field[0] - sign * coef_imag * field[1]
    imag_part = coef_real * field[1] + sign * coef_imag * field[0]
    return jnp.stack([real_part, imag_part])


def reference(model, freq_sq, source, observed, receiver_depth):
    levels = jax.lax.broadcasted_iota(jnp.int32, model.shape, 2)
    onehot = (levels == receiver_depth[:, :, None]).astype(jnp.float32)
    weights = penalty * onehot
    fields = []
    gradient = jnp.zeros(model.shape, jnp.float32)
    for freq in range(NF):
        squared = freq_sq[freq]
        coef_real = 6.0 - squared * model
        coef_imag = attenuation * squared * model

        def forward(field):
            return apply_coef(coef_real, coef_imag, field, 1.0) - neighbours(field)

        def adjoint(field):
            return apply_coef(coef_real, coef_imag, field, -1.0) - neighbours(field)

        def normal(field):
            return adjoint(forward(field)) + weights * field

        rhs = adjoint(source[freq]) + weights * observed[freq][:, :, :, None]
        field = jnp.zeros_like(rhs)
        resid = rhs
        direction = rhs
        norm_now = jnp.sum(resid * resid)
        for sweep in range(ITERS):
            image = normal(direction)
            alpha = norm_now / jnp.sum(direction * image)
            field = field + alpha * direction
            resid = resid - alpha * image
            norm_next = jnp.sum(resid * resid)
            direction = resid + (norm_next / norm_now) * direction
            norm_now = norm_next
        misfit = forward(field) - source[freq]
        deriv_real = -squared
        deriv_imag = attenuation * squared
        wave_real = deriv_real * field[0] - deriv_imag * field[1]
        wave_imag = deriv_real * field[1] + deriv_imag * field[0]
        gradient = gradient + (wave_real * misfit[0] + wave_imag * misfit[1])
        fields.append(field)
    return jnp.stack(fields), gradient
```

```python
import functools

import jax
import jax.numpy as jnp
from jax import lax
from jax.experimental import pallas as pl
from jax.experimental.pallas import tpu as pltpu
from jax.sharding import PartitionSpec as P

MESH = pl.DeviceIdType.MESH
ATTENUATION = 0.2
PENALTY = 4.0
PAD = 8


def kernel(dims, model_h, fsq, src_h, obs_h, depth_h, field_o, grad_o,
           S, B, U, Q, PP, M, W, WO, OB, DP, HX, HY, YS, A1S, A1R, A2S, A2R, GS, GR,
           load_sem, hs_sem, hr_sem, a1s_sem, a1r_sem, a2s_sem, a2r_sem, gs_sem, gr_sem):
    GX, GY, XL, YL, NGC = dims
    PX, PY = XL + 2, YL + 2 * PAD
    NT = YL // 8
    XT = XL // 8
    N1 = GX * 2
    N2 = GY // 2
    gx = lax.axis_index("gx")
    gy = lax.axis_index("gy")
    af = lax.axis_index("af")

    loads = [
        pltpu.make_async_copy(depth_h, DP, load_sem.at[XL]),
        pltpu.make_async_copy(obs_h, OB, load_sem.at[XL + 1]),
        pltpu.make_async_copy(model_h, M, load_sem.at[XL + 2]),
    ] + [
        pltpu.make_async_copy(src_h.at[:, x], S.at[:, pl.ds((1 + x) * PY + PAD, YL), :], load_sem.at[x])
        for x in range(XL)
    ]
    for cp in loads:
        cp.start()

    def first(j):
        r = lax.rem(gx * 2 + lax.rem(gy, 2) + j, N1)
        return r // 2, (gy // 2) * 2 + lax.rem(r, 2)

    def second(j):
        return lax.rem(gy // 2 + j, N2) * 2 + lax.rem(gy, 2)

    barrier = pltpu.get_barrier_semaphore()
    for j in range(1, N1):
        px, py = first(j)
        pl.semaphore_signal(barrier, inc=1, device_id={"gx": px, "gy": py}, device_id_type=MESH)
    for j in range(1, N2):
        pl.semaphore_signal(barrier, inc=1, device_id={"gy": second(j)}, device_id_type=MESH)
    pl.semaphore_signal(barrier, inc=1, device_id={"af": 1 - af}, device_id_type=MESH)

    @pl.when(gy > 0)
    def _():
        pl.semaphore_signal(barrier, inc=1, device_id={"gy": gy - 1}, device_id_type=MESH)

    @pl.when(gy < GY - 1)
    def _():
        pl.semaphore_signal(barrier, inc=1, device_id={"gy": gy + 1}, device_id_type=MESH)

    zero = jnp.zeros((8, 128), jnp.float32)

    def clear_rows(x, _):
        o = pl.multiple_of(x * PY, 8)
        for ref in (S, B, U, Q):
            for c in range(4):
                ref[c, pl.ds(o, 8), :] = zero
                ref[c, pl.ds(o + PAD + YL, 8), :] = zero
        return 0

    lax.fori_loop(0, PX, clear_rows, 0)
    for ref in (S, B, U, Q):
        for c in range(4):
            for xx in (0, PX - 1):
                for t in range(NT):
                    ref[c, pl.ds(xx * PY + PAD + t * 8, 8), :] = zero

    for k in range(2):
        A1S[k] = zero

    def clear_halo(ref, side, count):
        for e in range(4):
            for c in range(4):
                for r in range(0, count, 8):
                    ref[e, side, c, pl.ds(r, 8), :] = zero

    for cond, ref, side, count in ((gx == 0, HX, 0, YL), (gx == GX - 1, HX, 1, YL),
                                   (gy == 0, HY, 0, XL), (gy == GY - 1, HY, 1, XL)):
        pl.when(cond)(functools.partial(clear_halo, ref, side, count))

    def copies(e, V):
        out = []
        plan = (
            (gy > 0, {"gy": gy - 1}, YS.at[e, 0], HY.at[e, 1], 2, 3),
            (gy < GY - 1, {"gy": gy + 1}, YS.at[e, 1], HY.at[e, 0], 3, 2),
            (gx > 0, {"gx": gx - 1}, V.at[:, pl.ds(PY + PAD, YL), :],
             HX.at[e, 1], 0, 1),
            (gx < GX - 1, {"gx": gx + 1}, V.at[:, pl.ds(XL * PY + PAD, YL), :],
             HX.at[e, 0], 1, 0),
        )
        for cond, dev, s, d, mine, theirs in plan:
            out.append((cond, pltpu.make_async_remote_copy(
                src_ref=s, dst_ref=d, send_sem=hs_sem.at[e, mine], recv_sem=hr_sem.at[e, theirs],
                device_id=dev, device_id_type=MESH)))
        return out

    def send(e, V):
        for side, yy in ((0, PAD), (1, PAD + YL - 1)):
            for c in range(4):
                for k in range(XT):
                    YS[e, side, c, pl.ds(k * 8, 8), :] = V[c, pl.ds((1 + 8 * k) * PY + yy, 8, stride=PY), :]
        for cond, cp in copies(e, V):
            pl.when(cond)(cp.start)

    def arrive(e, V):
        cps = copies(e, V)
        for (cond, _), (_, cp) in zip(cps, (cps[1], cps[0], cps[3], cps[2])):
            pl.when(cond)(cp.wait_recv)

    def drain(e, V):
        for cond, cp in copies(e, V):
            pl.when(cond)(cp.wait_send)

    lane = lax.broadcasted_iota(jnp.int32, (8, 128), 1)
    at_first = lane == 0
    at_last = lane == 127
    sq = [fsq[0], fsq[1]]

    def around(V, c, o):
        cen = V[c, pl.ds(o, 8), :]
        t = V[c, pl.ds(o - PY, 8), :] + V[c, pl.ds(o + PY, 8), :]
        t = t + (V[c, pl.ds(o - 1, 8), :] + V[c, pl.ds(o + 1, 8), :])
        lo = jnp.where(at_first, 0.0, pltpu.roll(cen, 1, 1))
        hi = jnp.where(at_last, 0.0, pltpu.roll(cen, 127, 1))
        return cen, t + (lo + hi)

    def sweep(V, sign, finish, carry):
        def body(x, carry):
            o0 = pl.multiple_of(x * PY, 8)
            r0 = pl.multiple_of(x * YL, 8)
            for t in range(NT):
                m = M[pl.ds(r0 + t * 8, 8), :]
                for f in range(2):
                    k = sq[f] * m
                    cr = 6.0 - k
                    ci = (sign * ATTENUATION) * k
                    o = o0 + PY + PAD + t * 8
                    re, nre = around(V, 2 * f, o)
                    im, nim = around(V, 2 * f + 1, o)
                    out = (cr * re - ci * im - nre, cr * im + ci * re - nim)
                    carry = finish(f, o, r0 + t * 8, (re, im), out, carry)
            return carry
        return lax.fori_loop(0, XL, body, carry)

    def correct(e, rows, step, carry):
        for side in range(2):
            for c in range(4):
                for t in range(NT):
                    idx = rows(c, 1 + side * (XL - 1), PAD + t * 8, False)
                    carry = step(c // 2, idx, HX[e, side, c, pl.ds(t * 8, 8), :], carry)
        for side in range(2):
            for c in range(4):
                for k in range(XT):
                    idx = rows(c, 1 + 8 * k, PAD + side * (YL - 1), True)
                    carry = step(c // 2, idx, HY[e, side, c, pl.ds(k * 8, 8), :], carry)
        return carry

    def padded(c, xx, yy, strided):
        o = xx * PY + yy
        return c, pl.ds(o, 8, stride=PY) if strided else pl.ds(o, 8)

    def compact(c, xx, yy, strided):
        o = (xx - 1) * YL + yy - PAD
        return c, pl.ds(o, 8, stride=YL) if strided else pl.ds(o, 8)

    loads[0].wait()
    loads[1].wait()
    dt = jnp.transpose(jnp.concatenate(
        [DP[...].astype(jnp.float32), jnp.zeros((XL, 128 - YL), jnp.float32)], axis=1))
    ot = jnp.transpose(jnp.concatenate(
        [OB[...], jnp.zeros((4 * XL, 128 - YL), jnp.float32)], axis=1))
    lanef = lane.astype(jnp.float32)
    for x in range(XL):
        for t in range(NT):
            d = jnp.broadcast_to(dt[t * 8:t * 8 + 8, x:x + 1], (8, 128))
            w = jnp.where(lanef == d, PENALTY, 0.0)
            W[pl.ds(x * YL + t * 8, 8), :] = w
            for c in range(4):
                ob = jnp.broadcast_to(ot[t * 8:t * 8 + 8, c * XL + x:c * XL + x + 1], (8, 128))
                WO[c, pl.ds(x * YL + t * 8, 8), :] = w * ob

    for cp in loads[2:]:
        cp.wait()
    pl.semaphore_wait(barrier, N1 - 1 + N2 - 1 + 1 + (gy > 0).astype(jnp.int32) + (gy < GY - 1).astype(jnp.int32))
    send(0, S)

    def finish_b(f, o, r, cen, out, carry):
        acc = carry[f]
        for c in range(2):
            v = out[c] + WO[2 * f + c, pl.ds(r, 8), :]
            B[2 * f + c, pl.ds(o, 8), :] = v
            acc = acc + v * v
        return tuple(acc if i == f else carry[i] for i in range(2))

    def fix_field(ref, rows_of):
        def step(f, idx, h, carry):
            old = ref[idx[0], idx[1], :]
            new = old - h
            ref[idx[0], idx[1], :] = new
            d = h * (h - 2.0 * old)
            return tuple(carry[i] + d if i == f else carry[i] for i in range(2))
        return step

    rr = sweep(S, -1.0, finish_b, (zero, zero))
    arrive(0, S)
    rr = correct(0, padded, fix_field(B, padded), rr)
    send(1, B)

    def finish_u(f, o, r, cen, out, carry):
        acc = carry[f]
        for c in range(2):
            U[2 * f + c, pl.ds(o, 8), :] = out[c]
            acc = acc + out[c] * out[c]
        return tuple(acc if i == f else carry[i] for i in range(2))

    dq = sweep(B, 1.0, finish_u, (zero, zero))
    arrive(1, B)
    dq = correct(1, padded, fix_field(U, padded), dq)
    send(2, U)

    def finish_q(f, o, r, cen, out, carry):
        acc = carry[f]
        w = W[pl.ds(r, 8), :]
        for c in range(2):
            b = B[2 * f + c, pl.ds(o, 8), :]
            wb = w * b
            Q[2 * f + c, pl.ds(o, 8), :] = out[c] + wb
            acc = acc + wb * b
        return tuple(acc if i == f else carry[i] for i in range(2))

    dq = sweep(U, -1.0, finish_q, dq)

    def reduce_first(k, parts):
        for i, v in enumerate(parts):
            A1S[k, pl.ds(i, 1), :] = jnp.sum(v, axis=0, keepdims=True)
        for j in range(1, N1):
            px, py = first(j)
            pltpu.make_async_remote_copy(
                src_ref=A1S.at[k], dst_ref=A1R.at[k, N1 - j], send_sem=a1s_sem.at[k, j], recv_sem=a1r_sem.at[k, N1 - j],
                device_id={"gx": px, "gy": py}, device_id_type=MESH).start()

    def first_copy(k, j):
        px, py = first(j)
        return pltpu.make_async_remote_copy(
            src_ref=A1S.at[k], dst_ref=A1R.at[k, j], send_sem=a1s_sem.at[k, j], recv_sem=a1r_sem.at[k, j],
            device_id={"gx": px, "gy": py}, device_id_type=MESH)

    def second_copy(k, j, slot):
        return pltpu.make_async_remote_copy(
            src_ref=A2S.at[k], dst_ref=A2R.at[k, slot], send_sem=a2s_sem.at[k, j], recv_sem=a2r_sem.at[k, slot],
            device_id={"gy": second(j)}, device_id_type=MESH)

    def reduce_second(k):
        total = A1S[k]
        for j in range(1, N1):
            first_copy(k, j).wait_recv()
        for j in range(1, N1):
            total = total + A1R[k, j]
        A2S[k] = total
        for j in range(1, N2):
            second_copy(k, j, N2 - j).start()

    def reduce_end(k):
        total = A2S[k]
        for j in range(1, N2):
            second_copy(k, j, j).wait_recv()
        for j in range(1, N2):
            total = total + A2R[k, j]
        return jnp.broadcast_to(jnp.sum(total, axis=1, keepdims=True), (8, 128))

    def row(tile, i):
        return jnp.broadcast_to(tile[i:i + 1, :], (8, 128))

    reduce_first(0, (rr[0], rr[1], dq[0], dq[1]))

    arrive(2, U)

    def fix_plain(ref):
        def step(f, idx, h, carry):
            ref[idx[0], idx[1], :] = ref[idx[0], idx[1], :] - h
            return carry
        return step

    correct(2, padded, fix_plain(Q), 0)
    send(3, Q)
    reduce_second(0)

    def finish_p(f, o, r, cen, out, carry):
        for c in range(2):
            PP[2 * f + c, pl.ds(r, 8), :] = out[c]
        return carry

    sweep(Q, 1.0, finish_p, 0)
    sums = reduce_end(0)
    norm0 = [row(sums, f) for f in range(2)]
    curv0 = [row(sums, 2 + f) for f in range(2)]
    alpha0 = [norm0[f] / curv0[f] for f in range(2)]
    arrive(3, Q)
    correct(3, compact, fix_plain(PP), 0)

    def tally(x, carry):
        o0 = pl.multiple_of(x * PY, 8)
        r0 = pl.multiple_of(x * YL, 8)
        carry = list(carry)
        for t in range(NT):
            w = W[pl.ds(r0 + t * 8, 8), :]
            for f in range(2):
                for c in range(2):
                    off = PY + PAD + t * 8
                    q = Q[2 * f + c, pl.ds(o0 + off, 8), :]
                    r1 = B[2 * f + c, pl.ds(o0 + off, 8), :] - alpha0[f] * q
                    ar = U[2 * f + c, pl.ds(o0 + off, 8), :] - alpha0[f] * PP[2 * f + c, pl.ds(r0 + t * 8, 8), :]
                    r2 = r1 * r1
                    carry[f] = carry[f] + r2
                    carry[2 + f] = carry[2 + f] + (ar * ar + w * r2)
                    carry[4 + f] = carry[4 + f] + r1 * q
        return tuple(carry)

    tallies = lax.fori_loop(0, XL, tally, (zero,) * 6)
    reduce_first(1, tallies)
    reduce_second(1)
    sums = reduce_end(1)

    cb, cq = [], []
    for f in range(2):
        norm1 = row(sums, f)
        beta = norm1 / norm0[f]
        curv1 = row(sums, 2 + f) + (2.0 * beta) * row(sums, 4 + f) + (beta * beta) * curv0[f]
        alpha1 = norm1 / curv1
        cb.append(alpha0[f] + alpha1 * (1.0 + beta))
        cq.append(-(alpha0[f] * alpha1))

    GROWS = XL * YL // NGC
    def grad_copy(g):
        return pltpu.make_async_remote_copy(
            src_ref=GS.at[pl.ds(g * GROWS, GROWS), :], dst_ref=GR.at[pl.ds(g * GROWS, GROWS), :],
            send_sem=gs_sem.at[g], recv_sem=gr_sem.at[g], device_id={"af": 1 - af}, device_id_type=MESH)

    def outputs(x, _):
        o0 = pl.multiple_of(x * PY, 8)
        r0 = pl.multiple_of(x * YL, 8)
        for t in range(NT):
            g = zero
            for f in range(2):
                fld, mis = [], []
                for c in range(2):
                    off = PY + PAD + t * 8
                    ro = (2 * f + c) * XL * YL + r0 + t * 8
                    v = cb[f] * B[2 * f + c, pl.ds(o0 + off, 8), :] + cq[f] * Q[2 * f + c, pl.ds(o0 + off, 8), :]
                    field_o[pl.ds(ro, 8), :] = v
                    fld.append(v)
                    mis.append(cb[f] * U[2 * f + c, pl.ds(o0 + off, 8), :] + cq[f] * PP[2 * f + c, pl.ds(r0 + t * 8, 8), :] - S[2 * f + c, pl.ds(o0 + off, 8), :])
                wr = -fld[0] - ATTENUATION * fld[1]
                wi = ATTENUATION * fld[0] - fld[1]
                g = g + sq[f] * (wr * mis[0] + wi * mis[1])
            GS[pl.ds(r0 + t * 8, 8), :] = g
        return 0

    for g in range(NGC):
        lax.fori_loop(g * (XL // NGC), (g + 1) * (XL // NGC), outputs, 0)
        grad_copy(g).start()

    for g in range(NGC):
        grad_copy(g).wait_recv()

        def add(i, _):
            o = pl.multiple_of(i * 8, 8)
            grad_o[pl.ds(o, 8), :] = GS[pl.ds(o, 8), :] + GR[pl.ds(o, 8), :]
            return 0

        lax.fori_loop(g * GROWS // 8, (g + 1) * GROWS // 8, add, 0)

    for g in range(NGC):
        grad_copy(g).wait_send()
    for e, V in enumerate((S, B, U, Q)):
        drain(e, V)
    for k in range(2):
        for j in range(1, N1):
            first_copy(k, j).wait_send()
        for j in range(1, N2):
            second_copy(k, j, j).wait_send()


def solution(mesh):
    GX, GY = mesh.shape["gx"], mesh.shape["gy"]

    def on_device(model, freq_sq, source, observed, receiver_depth):
        XL, YL, ZL = model.shape
        PX, PY = XL + 2, YL + 2 * PAD
        f32 = jnp.float32
        N1, N2 = GX * 2, GY // 2
        NGC = 4
        big = pltpu.VMEM((4, PX * PY, ZL), f32)
        col = pltpu.VMEM((XL * YL, ZL), f32)
        dma = pltpu.SemaphoreType.DMA
        field, grad = pl.pallas_call(
            functools.partial(kernel, (GX, GY, XL, YL, NGC)),
            out_shape=(jax.ShapeDtypeStruct((4 * XL * YL, ZL), f32),
                       jax.ShapeDtypeStruct((XL * YL, ZL), f32)),
            in_specs=[pl.BlockSpec(memory_space=pl.ANY),
                      pl.BlockSpec(memory_space=pltpu.SMEM),
                      pl.BlockSpec(memory_space=pl.ANY),
                      pl.BlockSpec(memory_space=pl.ANY),
                      pl.BlockSpec(memory_space=pl.ANY)],
            out_specs=(pl.BlockSpec(memory_space=pltpu.VMEM),) * 2,
            scratch_shapes=[
                big, big, big, big,
                pltpu.VMEM((4, XL * YL, ZL), f32),
                col, col,
                pltpu.VMEM((4, XL * YL, ZL), f32),
                pltpu.VMEM((4 * XL, YL), f32),
                pltpu.VMEM((XL, YL), jnp.int32),
                pltpu.VMEM((4, 2, 4, YL, ZL), f32),
                pltpu.VMEM((4, 2, 4, XL, ZL), f32),
                pltpu.VMEM((4, 2, 4, XL, ZL), f32),
                pltpu.VMEM((2, 8, ZL), f32),
                pltpu.VMEM((2, N1, 8, ZL), f32),
                pltpu.VMEM((2, 8, ZL), f32),
                pltpu.VMEM((2, N2, 8, ZL), f32),
                col, col,
                dma((XL + 3,)), dma((4, 4)), dma((4, 4)),
                dma((2, N1)), dma((2, N1)), dma((2, N2)), dma((2, N2)),
                dma((NGC,)), dma((NGC,)),
            ],
            compiler_params=pltpu.CompilerParams(collective_id=0, has_side_effects=True),
        )(model.reshape(XL * YL, ZL), freq_sq, source.reshape(4, XL, YL, ZL),
          observed.reshape(4 * XL, YL), receiver_depth)
        return field.reshape(2, 2, XL, YL, ZL), grad.reshape(XL, YL, ZL)

    in_specs = (
        P("gx", "gy", None),
        P("af"),
        P("af", None, "gx", "gy", None),
        P("af", None, "gx", "gy"),
        P("gx", "gy"),
    )
    out_specs = (P("af", None, "gx", "gy", None), P("gx", "gy", None))
    return jax.shard_map(
        on_device, mesh=mesh, in_specs=in_specs, out_specs=out_specs, check_vma=False
    )
```

```python
import functools

import jax
import jax.numpy as jnp
from jax import lax
from jax.experimental import pallas as pl
from jax.experimental.pallas import tpu as pltpu
from jax.sharding import PartitionSpec as P

MESH = pl.DeviceIdType.MESH
ATTENUATION = 0.2
PENALTY = 4.0


def kernel(dims, model_h, fsq, src_h, obs_h, depth_h, field_o, grad_o,
           S, B, U, Q, PP, M, W, WO, OB, DP, HX, HY, YS, A1R, A2R, GS, GR,
           load_sem, hs_sem, hr_sem, a1s_sem, a1r_sem, a2s_sem, a2r_sem, tok_sem, gs_sem, gr_sem):
    GX, GY, XL, YL, NGC = dims
    PX = XL + 2
    NT = YL // 8
    XT = XL // 8
    N1 = GX * 2
    N2 = GY // 2
    gx = lax.axis_index("gx")
    gy = lax.axis_index("gy")
    af = lax.axis_index("af")

    def first(j):
        r = lax.rem(gx * 2 + lax.rem(gy, 2) + j, N1)
        return r // 2, (gy // 2) * 2 + lax.rem(r, 2)

    def second(j):
        return lax.rem(gy // 2 + j, N2) * 2 + lax.rem(gy, 2)

    def axis_peer(n, sign, axis):
        at, size, name = ((gx, GX, "gx"), (gy, GY, "gy"))[axis]
        return (at >= n, {name: at - n}) if sign < 0 else (at < size - n, {name: at + n})

    barrier = pltpu.get_barrier_semaphore()
    pl.semaphore_signal(barrier, inc=1, device_id={"af": 1 - af}, device_id_type=MESH)
    peers = jnp.int32(1)
    for axis in range(2):
        for sign in (-1, 1):
            cond, dev = axis_peer(1, sign, axis)
            peers = peers + cond.astype(jnp.int32)

            @pl.when(cond)
            def _():
                pl.semaphore_signal(barrier, inc=1, device_id=dev, device_id_type=MESH)

    def tell(r, n):
        for axis in range(2):
            for sign in (-1, 1):
                cond, dev = axis_peer(n, sign, axis)

                @pl.when(cond)
                def _():
                    pl.semaphore_signal(tok_sem.at[r, 2 * axis + (sign < 0)], inc=1, device_id=dev,
                                        device_id_type=MESH)

    def told(r, n):
        for axis in range(2):
            for sign in (-1, 1):
                cond, dev = axis_peer(n, sign, axis)

                @pl.when(cond)
                def _():
                    pl.semaphore_wait(tok_sem.at[r, 2 * axis + (sign > 0)], 1)

    loads = [
        pltpu.make_async_copy(depth_h, DP, load_sem.at[4]),
        pltpu.make_async_copy(obs_h, OB, load_sem.at[5]),
        pltpu.make_async_copy(model_h, M, load_sem.at[6]),
    ] + [
        pltpu.make_async_copy(src_h.at[c], S.at[c, pl.ds(YL, XL * YL), :], load_sem.at[c]) for c in range(4)
    ]
    for cp in loads:
        cp.start()

    zero = jnp.zeros((8, 128), jnp.float32)

    for ref in (S, B, U, Q):
        for c in range(4):
            for xx in (0, PX - 1):
                for t in range(NT):
                    ref[c, pl.ds(xx * YL + t * 8, 8), :] = zero

    def clear_halo(ref, side, count):
        for e in range(4):
            for c in range(4):
                for r in range(0, count, 8):
                    ref[e, side, c, pl.ds(r, 8), :] = zero

    for cond, ref, side, count in ((gx == 0, HX, 0, YL), (gx == GX - 1, HX, 1, YL),
                                   (gy == 0, HY, 0, XL), (gy == GY - 1, HY, 1, XL)):
        pl.when(cond)(functools.partial(clear_halo, ref, side, count))

    def copies(e, V):
        out = []
        plan = (
            (gy > 0, {"gy": gy - 1}, YS.at[e, 0], HY.at[e, 1], 2, 3),
            (gy < GY - 1, {"gy": gy + 1}, YS.at[e, 1], HY.at[e, 0], 3, 2),
            (gx > 0, {"gx": gx - 1}, V.at[:, pl.ds(YL, YL), :],
             HX.at[e, 1], 0, 1),
            (gx < GX - 1, {"gx": gx + 1}, V.at[:, pl.ds(XL * YL, YL), :],
             HX.at[e, 0], 1, 0),
        )
        for cond, dev, s, d, mine, theirs in plan:
            out.append((cond, pltpu.make_async_remote_copy(
                src_ref=s, dst_ref=d, send_sem=hs_sem.at[e, mine], recv_sem=hr_sem.at[e, theirs],
                device_id=dev, device_id_type=MESH)))
        return out

    def send(e, V):
        for side, yy in ((0, 0), (1, YL - 1)):
            for c in range(4):
                for k in range(XT):
                    YS[e, side, c, pl.ds(k * 8, 8), :] = V[c, pl.ds((1 + 8 * k) * YL + yy, 8, stride=YL), :]
        for cond, cp in copies(e, V):
            pl.when(cond)(cp.start)

    def arrive(e, V):
        cps = copies(e, V)
        for (cond, _), (_, cp) in zip(cps, (cps[1], cps[0], cps[3], cps[2])):
            pl.when(cond)(cp.wait_recv)

    def drain(e, V):
        for cond, cp in copies(e, V):
            pl.when(cond)(cp.wait_send)

    lane = lax.broadcasted_iota(jnp.int32, (8, 128), 1)
    at_first = lane == 0
    at_last = lane == 127
    sq = [fsq[0], fsq[1]]

    sub = lax.broadcasted_iota(jnp.int32, (8, 128), 0)
    UN = 2

    def around(V, c, o, t):
        cen = V[c, pl.ds(o, 8), :]
        total = V[c, pl.ds(o - YL, 8), :] + V[c, pl.ds(o + YL, 8), :]
        ym, yp = V[c, pl.ds(o - 1, 8), :], V[c, pl.ds(o + 1, 8), :]
        if t == 0:
            ym = jnp.where(sub == 0, 0.0, ym)
        if t == NT - 1:
            yp = jnp.where(sub == 7, 0.0, yp)
        total = total + (ym + yp)
        lo = jnp.where(at_first, 0.0, pltpu.roll(cen, 1, 1))
        hi = jnp.where(at_last, 0.0, pltpu.roll(cen, 127, 1))
        return cen, total + (lo + hi)

    def sweep(V, sign, finish, carry):
        def body(i, carry):
            for p in range(UN):
                r0 = pl.multiple_of(i * (UN * YL), 8) + p * YL
                for t in range(NT):
                    m = M[pl.ds(r0 + t * 8, 8), :]
                    for f in range(2):
                        k = sq[f] * m
                        cr = 6.0 - k
                        ci = (sign * ATTENUATION) * k
                        o = r0 + YL + t * 8
                        re, nre = around(V, 2 * f, o, t)
                        im, nim = around(V, 2 * f + 1, o, t)
                        out = (cr * re - ci * im - nre, cr * im + ci * re - nim)
                        carry = finish(f, o, r0 + t * 8, (re, im), out, carry)
            return carry
        return lax.fori_loop(0, XL // UN, body, carry)

    def correct(e, rows, step, carry):
        for side in range(2):
            for c in range(4):
                for t in range(NT):
                    idx = rows(c, 1 + side * (XL - 1), t * 8, False)
                    carry = step(c // 2, idx, HX[e, side, c, pl.ds(t * 8, 8), :], carry)
        for side in range(2):
            for c in range(4):
                for k in range(XT):
                    idx = rows(c, 1 + 8 * k, side * (YL - 1), True)
                    carry = step(c // 2, idx, HY[e, side, c, pl.ds(k * 8, 8), :], carry)
        return carry

    def padded(c, xx, yy, strided):
        o = xx * YL + yy
        return c, pl.ds(o, 8, stride=YL) if strided else pl.ds(o, 8)

    def compact(c, xx, yy, strided):
        return padded(c, xx - 1, yy, strided)

    loads[0].wait()
    loads[1].wait()
    dt = jnp.transpose(jnp.concatenate(
        [DP[...].astype(jnp.float32), jnp.zeros((XL, 128 - YL), jnp.float32)], axis=1))
    ot = jnp.transpose(jnp.concatenate(
        [OB[...], jnp.zeros((4 * XL, 128 - YL), jnp.float32)], axis=1))
    lanef = lane.astype(jnp.float32)
    for x in range(XL):
        for t in range(NT):
            d = jnp.broadcast_to(dt[t * 8:t * 8 + 8, x:x + 1], (8, 128))
            w = jnp.where(lanef == d, PENALTY, 0.0)
            W[pl.ds(x * YL + t * 8, 8), :] = w
            for c in range(4):
                ob = jnp.broadcast_to(ot[t * 8:t * 8 + 8, c * XL + x:c * XL + x + 1], (8, 128))
                WO[c, pl.ds(x * YL + t * 8, 8), :] = w * ob

    for cp in loads[2:]:
        cp.wait()
    pl.semaphore_wait(barrier, peers)
    send(0, S)

    def finish_b(f, o, r, cen, out, carry):
        acc = carry[f]
        for c in range(2):
            v = out[c] + WO[2 * f + c, pl.ds(r, 8), :]
            B[2 * f + c, pl.ds(o, 8), :] = v
            acc = acc + v * v
        return tuple(acc if i == f else carry[i] for i in range(2))

    def fix_field(ref):
        def step(f, idx, h, carry):
            old = ref[idx[0], idx[1], :]
            new = old - h
            ref[idx[0], idx[1], :] = new
            d = h * (h - 2.0 * old)
            return tuple(carry[i] + d if i == f else carry[i] for i in range(2))
        return step

    rr = sweep(S, -1.0, finish_b, (zero, zero))
    arrive(0, S)
    rr = correct(0, padded, fix_field(B), rr)
    send(1, B)
    tell(0, 2)

    def finish_u(f, o, r, cen, out, carry):
        acc = carry[f]
        for c in range(2):
            U[2 * f + c, pl.ds(o, 8), :] = out[c]
            acc = acc + out[c] * out[c]
        return tuple(acc if i == f else carry[i] for i in range(2))

    dq = sweep(B, 1.0, finish_u, (zero, zero))
    arrive(1, B)
    dq = correct(1, padded, fix_field(U), dq)
    send(2, U)
    told(0, 2)
    tell(1, 4)

    def finish_q(f, o, r, cen, out, carry):
        dq, qq = carry[f], carry[2 + f]
        w = W[pl.ds(r, 8), :]
        for c in range(2):
            b = B[2 * f + c, pl.ds(o, 8), :]
            wb = w * b
            v = out[c] + wb
            Q[2 * f + c, pl.ds(o, 8), :] = v
            dq = dq + wb * b
            qq = qq + v * v
        carry = list(carry)
        carry[f], carry[2 + f] = dq, qq
        return tuple(carry)

    carry = sweep(U, -1.0, finish_q, tuple(dq) + (zero, zero))
    dq, qq = carry[:2], carry[2:]
    arrive(2, U)
    qq = correct(2, padded, fix_field(Q), qq)
    send(3, Q)
    told(1, 4)
    tell(2, 8)

    def finish_p(f, o, r, cen, out, carry):
        acc = carry[f]
        w = W[pl.ds(r, 8), :]
        for c in range(2):
            PP[2 * f + c, pl.ds(r, 8), :] = out[c]
            acc = acc + (out[c] * out[c] + w * (cen[c] * cen[c]))
        return tuple(acc if i == f else carry[i] for i in range(2))

    qmq = sweep(Q, 1.0, finish_p, (zero, zero))
    arrive(3, Q)
    qmq = correct(3, compact, fix_field(PP), qmq)
    told(2, 8)

    group = lane // 16

    def first_copy(j, slot):
        px, py = first(j)
        return pltpu.make_async_remote_copy(
            src_ref=A1R.at[pl.ds(0, 1), :], dst_ref=A1R.at[pl.ds(slot, 1), :],
            send_sem=a1s_sem.at[j], recv_sem=a1r_sem.at[slot],
            device_id={"gx": px, "gy": py}, device_id_type=MESH)

    def second_copy(j, slot):
        return pltpu.make_async_remote_copy(
            src_ref=A2R.at[pl.ds(0, 1), :], dst_ref=A2R.at[pl.ds(slot, 1), :],
            send_sem=a2s_sem.at[j], recv_sem=a2r_sem.at[slot],
            device_id={"gy": second(j)}, device_id_type=MESH)

    def reduce_first(parts):
        mix = zero
        for i, v in enumerate(parts):
            for shift in (64, 32, 16):
                v = v + pltpu.roll(v, shift, 1)
            mix = jnp.where(group == i, v, mix)
        A1R[pl.ds(0, 1), :] = jnp.sum(mix, axis=0, keepdims=True)
        for j in range(1, N1):
            first_copy(j, N1 - j).start()

    def reduce_second():
        for j in range(1, N1):
            first_copy(j, j).wait_recv()
        A2R[pl.ds(0, 1), :] = jnp.sum(A1R[...], axis=0, keepdims=True)
        for j in range(1, N2):
            second_copy(j, N2 - j).start()

    def reduce_end():
        for j in range(1, N2):
            second_copy(j, j).wait_recv()
        v = jnp.broadcast_to(jnp.sum(A2R[...], axis=0, keepdims=True), (8, 128))
        for shift in (8, 4, 2, 1):
            v = v + pltpu.roll(v, 128 - shift, 1)
        return v

    def reduce_drain():
        for j in range(1, N1):
            first_copy(j, j).wait_send()
        for j in range(1, N2):
            second_copy(j, j).wait_send()

    def row(sums, i):
        return jnp.broadcast_to(sums[:, 16 * i:16 * i + 1], (8, 128))

    reduce_first((rr[0], rr[1], dq[0], dq[1], qq[0], qq[1], qmq[0], qmq[1]))
    for e, V in enumerate((S, B, U, Q)):
        drain(e, V)
    reduce_second()
    sums = reduce_end()

    cb, cq = [], []
    for f in range(2):
        norm0, curv0, qq0, qmq0 = (row(sums, 2 * i + f) for i in range(4))
        alpha0 = norm0 / curv0
        norm1 = norm0 - alpha0 * (2.0 * curv0 - alpha0 * qq0)
        beta = norm1 / norm0
        rq = curv0 - alpha0 * qq0
        rmr = curv0 - alpha0 * (2.0 * qq0 - alpha0 * qmq0)
        alpha1 = norm1 / (rmr + beta * (2.0 * rq + beta * curv0))
        cb.append(alpha0 + alpha1 * (1.0 + beta))
        cq.append(-(alpha0 * alpha1))

    GROWS = XL * YL // NGC
    def grad_copy(g):
        return pltpu.make_async_remote_copy(
            src_ref=GS.at[pl.ds(g * GROWS, GROWS), :], dst_ref=GR.at[pl.ds(g * GROWS, GROWS), :],
            send_sem=gs_sem.at[g], recv_sem=gr_sem.at[g], device_id={"af": 1 - af}, device_id_type=MESH)

    def outputs(i, _):
        for p in range(UN):
            r0 = pl.multiple_of(i * (UN * YL), 8) + p * YL
            for t in range(NT):
                r = r0 + t * 8
                g = zero
                for f in range(2):
                    fld, mis = [], []
                    for c in range(2):
                        n = 2 * f + c
                        v = cb[f] * B[n, pl.ds(r + YL, 8), :] + cq[f] * Q[n, pl.ds(r + YL, 8), :]
                        field_o[n, pl.ds(r, 8), :] = v
                        fld.append(v)
                        mis.append(cb[f] * U[n, pl.ds(r + YL, 8), :] + cq[f] * PP[n, pl.ds(r, 8), :]
                                   - S[n, pl.ds(r + YL, 8), :])
                    wr = -fld[0] - ATTENUATION * fld[1]
                    wi = ATTENUATION * fld[0] - fld[1]
                    g = g + sq[f] * (wr * mis[0] + wi * mis[1])
                GS[pl.ds(r, 8), :] = g
        return 0

    for g in range(NGC):
        lax.fori_loop(g * (XL // NGC // UN), (g + 1) * (XL // NGC // UN), outputs, 0)
        grad_copy(g).start()

    for g in range(NGC):
        grad_copy(g).wait_recv()

        def add(i, _):
            for n in range(8):
                o = pl.multiple_of(i * 64, 8) + n * 8
                grad_o[pl.ds(o, 8), :] = GS[pl.ds(o, 8), :] + GR[pl.ds(o, 8), :]
            return 0

        lax.fori_loop(g * GROWS // 64, (g + 1) * GROWS // 64, add, 0)

    for g in range(NGC):
        grad_copy(g).wait_send()
    reduce_drain()


def solution(mesh):
    GX, GY = mesh.shape["gx"], mesh.shape["gy"]

    def on_device(model, freq_sq, source, observed, receiver_depth):
        XL, YL, ZL = model.shape
        PX = XL + 2
        f32 = jnp.float32
        N1, N2 = GX * 2, GY // 2
        NGC = 4
        big = pltpu.VMEM((4, PX * YL, ZL), f32)
        col = pltpu.VMEM((XL * YL, ZL), f32)
        dma = pltpu.SemaphoreType.DMA
        field, grad = pl.pallas_call(
            functools.partial(kernel, (GX, GY, XL, YL, NGC)),
            out_shape=(jax.ShapeDtypeStruct((4, XL * YL, ZL), f32),
                       jax.ShapeDtypeStruct((XL * YL, ZL), f32)),
            in_specs=[pl.BlockSpec(memory_space=pltpu.HBM),
                      pl.BlockSpec(memory_space=pltpu.SMEM),
                      pl.BlockSpec(memory_space=pltpu.HBM),
                      pl.BlockSpec(memory_space=pltpu.HBM),
                      pl.BlockSpec(memory_space=pltpu.HBM)],
            out_specs=(pl.BlockSpec(memory_space=pltpu.VMEM),) * 2,
            scratch_shapes=[
                big, big, big, big,
                pltpu.VMEM((4, XL * YL, ZL), f32),
                col, col,
                pltpu.VMEM((4, XL * YL, ZL), f32),
                pltpu.VMEM((4 * XL, YL), f32),
                pltpu.VMEM((XL, YL), jnp.int32),
                pltpu.VMEM((4, 2, 4, YL, ZL), f32),
                pltpu.VMEM((4, 2, 4, XL, ZL), f32),
                pltpu.VMEM((4, 2, 4, XL, ZL), f32),
                pltpu.VMEM((N1, ZL), f32),
                pltpu.VMEM((N2, ZL), f32),
                col, col,
                dma((7,)), dma((4, 4)), dma((4, 4)),
                dma((N1,)), dma((N1,)), dma((N2,)), dma((N2,)),
                pltpu.SemaphoreType.REGULAR((3, 4)),
                dma((NGC,)), dma((NGC,)),
            ],
            compiler_params=pltpu.CompilerParams(
                collective_id=0, has_side_effects=True, vmem_limit_bytes=26 * 2**20),
        )(*[pltpu.with_memory_space_constraint(a, pltpu.HBM) for a in (
            model.reshape(XL * YL, ZL), freq_sq, source.reshape(4, XL * YL, ZL),
            observed.reshape(4 * XL, YL), receiver_depth)])
        return field.reshape(2, 2, XL, YL, ZL), grad.reshape(XL, YL, ZL)

    in_specs = (
        P("gx", "gy", None),
        P("af"),
        P("af", None, "gx", "gy", None),
        P("af", None, "gx", "gy"),
        P("gx", "gy"),
    )
    out_specs = (P("af", None, "gx", "gy", None), P("gx", "gy", None))
    return jax.shard_map(
        on_device, mesh=mesh, in_specs=in_specs, out_specs=out_specs, check_vma=False
    )
```

```python
import functools

import jax
import jax.numpy as jnp
from jax import lax
from jax.experimental import pallas as pl
from jax.experimental.pallas import tpu as pltpu
from jax.sharding import PartitionSpec as P

MESH = pl.DeviceIdType.MESH
ATTENUATION = 0.2
PENALTY = 4.0


def kernel(dims, model_h, fsq, src_h, obs_h, depth_h, field_o, grad_o,
           S, B, U, Q, PP, M, W, WO, OB, DP, X1, X2, Y1, Y2, YS, MX, MY, MYS, IS, IR, CS, CR, WH, WOH, BH,
           A1R, A2R, GS, GR,
           load_sem, hs_sem, hr_sem, ms_sem, mr_sem, cs_sem, cr_sem,
           a1s_sem, a1r_sem, a2s_sem, a2r_sem, tok_sem, gs_sem, gr_sem):
    GX, GY, XL, YL, NGC = dims
    PX = XL + 2
    NT = YL // 8
    XT = XL // 8
    N1 = GX * 2
    N2 = GY // 2
    gx = lax.axis_index("gx")
    gy = lax.axis_index("gy")
    af = lax.axis_index("af")

    def first(j):
        r = lax.rem(gx * 2 + lax.rem(gy, 2) + j, N1)
        return r // 2, (gy // 2) * 2 + lax.rem(r, 2)

    def second(j):
        return lax.rem(gy // 2 + j, N2) * 2 + lax.rem(gy, 2)

    def axis_peer(n, sign, axis):
        at, size, name = ((gx, GX, "gx"), (gy, GY, "gy"))[axis]
        return (at >= n, {name: at - n}) if sign < 0 else (at < size - n, {name: at + n})

    barrier = pltpu.get_barrier_semaphore()
    pl.semaphore_signal(barrier, inc=1, device_id={"af": 1 - af}, device_id_type=MESH)
    peers = jnp.int32(1)
    for axis in range(2):
        for sign in (-1, 1):
            cond, dev = axis_peer(1, sign, axis)
            peers = peers + cond.astype(jnp.int32)

            @pl.when(cond)
            def _():
                pl.semaphore_signal(barrier, inc=1, device_id=dev, device_id_type=MESH)

    def tell(r, n):
        for axis in range(2):
            for sign in (-1, 1):
                cond, dev = axis_peer(n, sign, axis)

                @pl.when(cond)
                def _():
                    pl.semaphore_signal(tok_sem.at[r, 2 * axis + (sign < 0)], inc=1, device_id=dev,
                                        device_id_type=MESH)

    def told(r, n):
        for axis in range(2):
            for sign in (-1, 1):
                cond, dev = axis_peer(n, sign, axis)

                @pl.when(cond)
                def _():
                    pl.semaphore_wait(tok_sem.at[r, 2 * axis + (sign > 0)], 1)

    loads = [
        pltpu.make_async_copy(depth_h, DP, load_sem.at[4]),
        pltpu.make_async_copy(obs_h, OB, load_sem.at[5]),
        pltpu.make_async_copy(model_h, M, load_sem.at[6]),
    ] + [
        pltpu.make_async_copy(src_h.at[c], S.at[c, pl.ds(YL, XL * YL), :], load_sem.at[c]) for c in range(4)
    ]
    for cp in loads:
        cp.start()

    zero = jnp.zeros((8, 128), jnp.float32)

    for ref in (S, B, U, Q):
        for c in range(4):
            for xx in (0, PX - 1):
                for t in range(NT):
                    ref[c, pl.ds(xx * YL + t * 8, 8), :] = zero

    def clear(ref, side, count):
        for e in range(2):
            for c in range(4):
                for r in range(0, count, 8):
                    ref[e, side, c, pl.ds(8 + r, 8), :] = zero

    has = ((gx > 0, gx < GX - 1), (gy > 0, gy < GY - 1))
    for side in range(2):
        pl.when(jnp.logical_not(has[0][side]))(functools.partial(clear, X1, side, YL))
        pl.when(jnp.logical_not(has[1][side]))(functools.partial(clear, Y1, side, XL))
    for sx in range(2):
        for sy in range(2):
            @pl.when(jnp.logical_not(jnp.logical_and(has[0][sx], has[1][sy])))
            def _():
                for e in range(2):
                    CR[e, 2 * sx + sy] = zero

    for face in range(4):
        @pl.when(jnp.logical_not(has[face // 2][face % 2]))
        def _():
            IR[face] = zero

    def remote(src, dst, ssem, rsem, dev):
        return pltpu.make_async_remote_copy(
            src_ref=src, dst_ref=dst, send_sem=ssem, recv_sem=rsem, device_id=dev, device_id_type=MESH)

    def face_dev(face):
        axis, side = face // 2, face % 2
        step = 2 * side - 1
        return has[axis][side], ({"gx": gx + step} if axis == 0 else {"gy": gy + step})

    def layer_copy(e, l, V, face):
        axis, side = face // 2, face % 2
        there = 1 - side
        if axis == 0:
            plane = l if side == 0 else XL - 1 - l
            src = V.at[:, pl.ds((1 + plane) * YL, YL), :]
            dst = X1.at[e, there, :, pl.ds(8, YL), :] if l == 0 else X2.at[e, there]
        else:
            src = YS.at[e, side, l]
            dst = Y1.at[e, there, :, pl.ds(8, XL), :] if l == 0 else Y2.at[e, there]
        cond, dev = face_dev(face)
        return cond, remote(src, dst, hs_sem.at[e, l, face], hr_sem.at[e, l, 2 * axis + there], dev)

    def model_copy(face):
        axis, side = face // 2, face % 2
        there = 1 - side
        if axis == 0:
            src, dst = M.at[pl.ds(side * (XL - 1) * YL, YL), :], MX.at[there]
        else:
            src, dst = MYS.at[side], MY.at[there]
        cond, dev = face_dev(face)
        return cond, remote(src, dst, ms_sem.at[0, face], mr_sem.at[0, 2 * axis + there], dev)

    def info_copy(face):
        axis, side = face // 2, face % 2
        there = 2 * axis + 1 - side
        cond, dev = face_dev(face)
        return cond, remote(IS.at[face], IR.at[there], ms_sem.at[1, face], mr_sem.at[1, there], dev)

    def corner_copy(e, k):
        sx, sy = k // 2, k % 2
        return jnp.logical_and(has[0][sx], has[1][sy]), remote(
            CS.at[e, k, pl.ds(0, 4), :], CR.at[e, 3 - k, pl.ds(0, 4), :], cs_sem.at[e, k], cr_sem.at[e, 3 - k],
            {"gx": gx + (2 * sx - 1), "gy": gy + (2 * sy - 1)})

    FACES = (2, 3, 0, 1)
    other = lambda face: face ^ 1

    def start_all(copies):
        for cond, cp in copies:
            pl.when(cond)(cp.start)

    def drain_all(copies):
        for cond, cp in copies:
            pl.when(cond)(cp.wait_send)

    def arrive_all(make, faces):
        for face in faces:
            cond, _ = face_dev(face)
            pl.when(cond)(make(other(face))[1].wait_recv)

    def arrive_layer(e, l, V):
        arrive_all(lambda face: layer_copy(e, l, V, face), FACES)

    def arrive_corners(e):
        for k in range(4):
            pl.when(jnp.logical_and(has[0][k // 2], has[1][k % 2]))(corner_copy(e, 3 - k)[1].wait_recv)
        for k in range(4):
            sx, sy = k // 2, k % 2
            for c in range(4):
                v = CR[e, k, pl.ds(c, 1), :]
                X1[e, sx, c, pl.ds(8 + YL if sy else 7, 1), :] = v
                Y1[e, sy, c, pl.ds(8 + XL if sx else 7, 1), :] = v

    def pack_layer(e, l, V):
        for side in range(2):
            y = l if side == 0 else YL - 1 - l
            for c in range(4):
                for k in range(XT):
                    YS[e, side, l, c, pl.ds(k * 8, 8), :] = V[c, pl.ds((1 + 8 * k) * YL + y, 8, stride=YL), :]

    def pack_corners(e, V):
        for k in range(4):
            o = (1 + (XL - 1) * (k // 2)) * YL + (YL - 1) * (k % 2)
            for c in range(4):
                CS[e, k, pl.ds(c, 1), :] = V[c, pl.ds(o, 1), :]

    lane = lax.broadcasted_iota(jnp.int32, (8, 128), 1)
    at_first = lane == 0
    at_last = lane == 127
    sq = [fsq[0], fsq[1]]

    sub = lax.broadcasted_iota(jnp.int32, (8, 128), 0)
    UN = 2

    def around(V, c, o, t):
        cen = V[c, pl.ds(o, 8), :]
        total = V[c, pl.ds(o - YL, 8), :] + V[c, pl.ds(o + YL, 8), :]
        ym, yp = V[c, pl.ds(o - 1, 8), :], V[c, pl.ds(o + 1, 8), :]
        if t == 0:
            ym = jnp.where(sub == 0, 0.0, ym)
        if t == NT - 1:
            yp = jnp.where(sub == 7, 0.0, yp)
        total = total + (ym + yp)
        lo = jnp.where(at_first, 0.0, pltpu.roll(cen, 1, 1))
        hi = jnp.where(at_last, 0.0, pltpu.roll(cen, 127, 1))
        return cen, total + (lo + hi)

    def coefs(f, m, sign):
        k = sq[f] * m
        return 6.0 - k, (sign * ATTENUATION) * k

    def tiles_of(V, sign, finish, r0, tiles, carry):
        for t in tiles:
            m = M[pl.ds(r0 + t * 8, 8), :]
            for f in range(2):
                cr, ci = coefs(f, m, sign)
                o = r0 + YL + t * 8
                re, nre = around(V, 2 * f, o, t)
                im, nim = around(V, 2 * f + 1, o, t)
                out = (cr * re - ci * im - nre, cr * im + ci * re - nim)
                carry = finish(f, o, r0 + t * 8, (re, im), out, carry)
        return carry

    def planes(V, sign, finish, carry, lo, hi, un, tiles):
        def body(i, carry):
            for p in range(un):
                r0 = pl.multiple_of(i * (un * YL), 8) + (lo + p) * YL
                carry = tiles_of(V, sign, finish, r0, tiles, carry)
            return carry
        if not tiles:
            return carry
        return lax.fori_loop(0, (hi - lo) // un, body, carry)

    def sweep(V, sign, finish, carry):
        return planes(V, sign, finish, carry, 0, XL, UN, range(NT))

    def sweep_inner(V, sign, finish, carry):
        return planes(V, sign, finish, carry, 2, XL - 2, 4, range(1, NT - 1))

    def sweep_outer(V, sign, finish, carry):
        carry = planes(V, sign, finish, carry, 2, XL - 2, 4, (0, NT - 1))
        def ends(i, carry):
            for p in range(2):
                r0 = pl.multiple_of(i * ((XL - 2) * YL), 8) + p * YL
                carry = tiles_of(V, sign, finish, r0, range(NT), carry)
            return carry
        return lax.fori_loop(0, 2, ends, carry)

    def strip(e, V, face, finish, carry):
        axis, side = face // 2, face % 2
        H1, H2, MH, L = (X1, X2, MX, YL) if axis == 0 else (Y1, Y2, MY, XL)
        for k in range(L // 8):
            m = MH[side, pl.ds(8 * k, 8), :]
            for f in range(2):
                cr, ci = coefs(f, m, -1.0)
                cen, nb = [], []
                for c in (2 * f, 2 * f + 1):
                    v = H1[e, side, c, pl.ds(8 + 8 * k, 8), :]
                    if axis == 0:
                        inward = V[c, pl.ds((1 + side * (XL - 1)) * YL + 8 * k, 8), :]
                    else:
                        inward = V[c, pl.ds((1 + 8 * k) * YL + side * (YL - 1), 8, stride=YL), :]
                    total = (H2[e, side, c, pl.ds(8 * k, 8), :] + inward) + (
                        H1[e, side, c, pl.ds(7 + 8 * k, 8), :] + H1[e, side, c, pl.ds(9 + 8 * k, 8), :])
                    lo = jnp.where(at_first, 0.0, pltpu.roll(v, 1, 1))
                    hi = jnp.where(at_last, 0.0, pltpu.roll(v, 127, 1))
                    cen.append(v)
                    nb.append(total + (lo + hi))
                out = (cr * cen[0] - ci * cen[1] - nb[0], cr * cen[1] + ci * cen[0] - nb[1])
                carry = finish(face, k, f, out, carry)
        return carry

    def on_face(rows, face, c, k):
        axis, side = face // 2, face % 2
        if axis == 0:
            return rows(c, 1 + side * (XL - 1), 8 * k, False)
        return rows(c, 1 + 8 * k, side * (YL - 1), True)

    def take(ref, idx, h, f, carry):
        old = ref[idx[0], idx[1], :]
        ref[idx[0], idx[1], :] = old - h
        d = h * (h - 2.0 * old)
        return tuple(carry[i] + d if i == f else carry[i] for i in range(2))

    def correct(e, ref, carry):
        for face in range(4):
            H1, L = (X1, YL) if face < 2 else (Y1, XL)
            for c in range(4):
                for k in range(L // 8):
                    h = H1[e, face % 2, c, pl.ds(8 + 8 * k, 8), :]
                    carry = take(ref, on_face(padded, face, c, k), h, c // 2, carry)
        return carry

    def padded(c, xx, yy, strided):
        o = xx * YL + yy
        return c, pl.ds(o, 8, stride=YL) if strided else pl.ds(o, 8)

    def compact(c, xx, yy, strided):
        return padded(c, xx - 1, yy, strided)

    loads[0].wait()
    loads[1].wait()
    dt = jnp.transpose(jnp.concatenate(
        [DP[...].astype(jnp.float32), jnp.zeros((XL, 128 - YL), jnp.float32)], axis=1))
    ot = jnp.transpose(jnp.concatenate(
        [OB[...], jnp.zeros((4 * XL, 128 - YL), jnp.float32)], axis=1))
    for face in range(4):
        IS[face] = zero
    for side in range(2):
        x, y = side * (XL - 1), side * (YL - 1)
        for c in range(4):
            IS[side, c:c + 1, 0:YL] = OB[c * XL + x:c * XL + x + 1, :]
        IS[side, 4:5, 0:YL] = DP[x:x + 1, :].astype(jnp.float32)
        IS[2 + side, 0:1, 0:4 * XL] = ot[y:y + 1, :]
        IS[2 + side, 1:2, 0:XL] = dt[y:y + 1, :]
    for cp in loads[2:]:
        cp.wait()
    for l in range(2):
        pack_layer(0, l, S)
    pack_corners(0, S)
    for side in range(2):
        for k in range(XT):
            MYS[side, pl.ds(8 * k, 8), :] = M[pl.ds(8 * k * YL + side * (YL - 1), 8, stride=YL), :]
    pl.semaphore_wait(barrier, peers)
    start_all([layer_copy(0, 0, S, face) for face in FACES])
    start_all([info_copy(face) for face in FACES])
    start_all([layer_copy(0, 1, S, face) for face in FACES])
    start_all([model_copy(face) for face in FACES])
    tell(0, 1)

    lanef = lane.astype(jnp.float32)
    for x in range(XL):
        for t in range(NT):
            d = jnp.broadcast_to(dt[t * 8:t * 8 + 8, x:x + 1], (8, 128))
            w = jnp.where(lanef == d, PENALTY, 0.0)
            W[pl.ds(x * YL + t * 8, 8), :] = w
            for c in range(4):
                ob = jnp.broadcast_to(ot[t * 8:t * 8 + 8, c * XL + x:c * XL + x + 1], (8, 128))
                WO[c, pl.ds(x * YL + t * 8, 8), :] = w * ob

    def finish_b(f, o, r, cen, out, carry):
        acc = carry[f]
        for c in range(2):
            v = out[c] + WO[2 * f + c, pl.ds(r, 8), :]
            B[2 * f + c, pl.ds(o, 8), :] = v
            acc = acc + v * v
        return tuple(acc if i == f else carry[i] for i in range(2))

    rr = sweep(S, -1.0, finish_b, (zero, zero))
    told(0, 1)
    start_all([corner_copy(0, k) for k in range(4)])
    tell(1, 2)

    def finish_u(f, o, r, cen, out, carry):
        acc = carry[f]
        for c in range(2):
            U[2 * f + c, pl.ds(o, 8), :] = out[c]
            acc = acc + out[c] * out[c]
        return tuple(acc if i == f else carry[i] for i in range(2))

    dq = sweep_inner(B, 1.0, finish_u, (zero, zero))
    arrive_layer(0, 0, S)
    rr = correct(0, B, rr)
    told(1, 2)
    tell(2, 4)
    dq = sweep_outer(B, 1.0, finish_u, dq)

    arrive_all(info_copy, FACES)
    it = jnp.transpose(jnp.concatenate(
        [IR[face] for face in range(4)] + [jnp.zeros((96, 128), jnp.float32)], axis=0))
    for face in range(4):
        L = YL if face < 2 else XL
        for k in range(L // 8):
            if face < 2:
                d = it[8 * k:8 * k + 8, 8 * face + 4:8 * face + 5]
                obs = [it[8 * k:8 * k + 8, 8 * face + c:8 * face + c + 1] for c in range(4)]
            else:
                d = it[8 * k:8 * k + 8, 8 * face + 1:8 * face + 2]
                obs = [it[c * XL + 8 * k:c * XL + 8 * k + 8, 8 * face:8 * face + 1] for c in range(4)]
            w = jnp.where(lanef == jnp.broadcast_to(d, (8, 128)), PENALTY, 0.0)
            WH[face, pl.ds(8 * k, 8), :] = w
            for c in range(4):
                WOH[face, c, pl.ds(8 * k, 8), :] = w * jnp.broadcast_to(obs[c], (8, 128))

    def finish_bh(face, k, f, out, carry):
        cond, _ = face_dev(face)
        for i in range(2):
            c = 2 * f + i
            v = jnp.where(cond, out[i] + WOH[face, c, pl.ds(8 * k, 8), :], 0.0)
            BH[face, c, pl.ds(8 * k, 8), :] = v
            carry = take(U, on_face(padded, face, c, k), v, f, carry)
        return carry

    arrive_all(model_copy, FACES)
    arrive_layer(0, 1, S)
    arrive_corners(0)
    for face in FACES:
        dq = strip(0, S, face, finish_bh, dq)
    pack_corners(1, U)
    for l in range(2):
        pack_layer(1, l, U)
    start_all([corner_copy(1, k) for k in range(4)])
    for l in range(2):
        start_all([layer_copy(1, l, U, face) for face in FACES])
    told(2, 4)
    tell(3, 8)

    def finish_q(f, o, r, cen, out, carry):
        dq, qq = carry[f], carry[2 + f]
        w = W[pl.ds(r, 8), :]
        for c in range(2):
            b = B[2 * f + c, pl.ds(o, 8), :]
            wb = w * b
            v = out[c] + wb
            Q[2 * f + c, pl.ds(o, 8), :] = v
            dq = dq + wb * b
            qq = qq + v * v
        carry = list(carry)
        carry[f], carry[2 + f] = dq, qq
        return tuple(carry)

    carry = sweep(U, -1.0, finish_q, tuple(dq) + (zero, zero))
    dq, qq = carry[:2], carry[2:]
    def finish_p(f, o, r, cen, out, carry):
        acc = carry[f]
        w = W[pl.ds(r, 8), :]
        for c in range(2):
            PP[2 * f + c, pl.ds(r, 8), :] = out[c]
            acc = acc + (out[c] * out[c] + w * (cen[c] * cen[c]))
        return tuple(acc if i == f else carry[i] for i in range(2))

    qmq = sweep_inner(Q, 1.0, finish_p, (zero, zero))
    arrive_layer(1, 0, U)
    qq = correct(1, Q, qq)
    told(3, 8)
    qmq = sweep_outer(Q, 1.0, finish_p, qmq)

    def finish_qh(face, k, f, out, carry):
        cond, _ = face_dev(face)
        w = WH[face, pl.ds(8 * k, 8), :]
        for i in range(2):
            c = 2 * f + i
            v = jnp.where(cond, out[i] + w * BH[face, c, pl.ds(8 * k, 8), :], 0.0)
            carry = take(PP, on_face(compact, face, c, k), v, f, carry)
        return carry

    arrive_layer(1, 1, U)
    arrive_corners(1)
    for face in FACES:
        qmq = strip(1, U, face, finish_qh, qmq)

    group = lane // 16

    def first_copy(j, slot):
        px, py = first(j)
        return pltpu.make_async_remote_copy(
            src_ref=A1R.at[pl.ds(0, 1), :], dst_ref=A1R.at[pl.ds(slot, 1), :],
            send_sem=a1s_sem.at[j], recv_sem=a1r_sem.at[slot],
            device_id={"gx": px, "gy": py}, device_id_type=MESH)

    def second_copy(j, slot):
        return pltpu.make_async_remote_copy(
            src_ref=A2R.at[pl.ds(0, 1), :], dst_ref=A2R.at[pl.ds(slot, 1), :],
            send_sem=a2s_sem.at[j], recv_sem=a2r_sem.at[slot],
            device_id={"gy": second(j)}, device_id_type=MESH)

    def reduce_first(parts):
        mix = zero
        for i, v in enumerate(parts):
            for shift in (64, 32, 16):
                v = v + pltpu.roll(v, shift, 1)
            mix = jnp.where(group == i, v, mix)
        A1R[pl.ds(0, 1), :] = jnp.sum(mix, axis=0, keepdims=True)
        for j in range(1, N1):
            first_copy(j, N1 - j).start()

    def reduce_second():
        for j in range(1, N1):
            first_copy(j, j).wait_recv()
        A2R[pl.ds(0, 1), :] = jnp.sum(A1R[...], axis=0, keepdims=True)
        for j in range(1, N2):
            second_copy(j, N2 - j).start()

    def reduce_end():
        for j in range(1, N2):
            second_copy(j, j).wait_recv()
        v = jnp.broadcast_to(jnp.sum(A2R[...], axis=0, keepdims=True), (8, 128))
        for shift in (8, 4, 2, 1):
            v = v + pltpu.roll(v, 128 - shift, 1)
        return v

    def reduce_drain():
        for j in range(1, N1):
            first_copy(j, j).wait_send()
        for j in range(1, N2):
            second_copy(j, j).wait_send()

    def row(sums, i):
        return jnp.broadcast_to(sums[:, 16 * i:16 * i + 1], (8, 128))

    reduce_first((rr[0], rr[1], dq[0], dq[1], qq[0], qq[1], qmq[0], qmq[1]))
    for e, V in ((0, S), (1, U)):
        for l in range(2):
            drain_all([layer_copy(e, l, V, face) for face in FACES])
        drain_all([corner_copy(e, k) for k in range(4)])
    drain_all([model_copy(face) for face in FACES])
    drain_all([info_copy(face) for face in FACES])
    reduce_second()
    sums = reduce_end()

    cb, cq = [], []
    for f in range(2):
        norm0, curv0, qq0, qmq0 = (row(sums, 2 * i + f) for i in range(4))
        alpha0 = norm0 / curv0
        norm1 = norm0 - alpha0 * (2.0 * curv0 - alpha0 * qq0)
        beta = norm1 / norm0
        rq = curv0 - alpha0 * qq0
        rmr = curv0 - alpha0 * (2.0 * qq0 - alpha0 * qmq0)
        alpha1 = norm1 / (rmr + beta * (2.0 * rq + beta * curv0))
        cb.append(alpha0 + alpha1 * (1.0 + beta))
        cq.append(-(alpha0 * alpha1))

    GROWS = XL * YL // NGC
    def grad_copy(g):
        return pltpu.make_async_remote_copy(
            src_ref=GS.at[pl.ds(g * GROWS, GROWS), :], dst_ref=GR.at[pl.ds(g * GROWS, GROWS), :],
            send_sem=gs_sem.at[g], recv_sem=gr_sem.at[g], device_id={"af": 1 - af}, device_id_type=MESH)

    def outputs(i, _):
        for p in range(UN):
            r0 = pl.multiple_of(i * (UN * YL), 8) + p * YL
            for t in range(NT):
                r = r0 + t * 8
                g = zero
                for f in range(2):
                    fld, mis = [], []
                    for c in range(2):
                        n = 2 * f + c
                        v = cb[f] * B[n, pl.ds(r + YL, 8), :] + cq[f] * Q[n, pl.ds(r + YL, 8), :]
                        field_o[n, pl.ds(r, 8), :] = v
                        fld.append(v)
                        mis.append(cb[f] * U[n, pl.ds(r + YL, 8), :] + cq[f] * PP[n, pl.ds(r, 8), :]
                                   - S[n, pl.ds(r + YL, 8), :])
                    wr = -fld[0] - ATTENUATION * fld[1]
                    wi = ATTENUATION * fld[0] - fld[1]
                    g = g + sq[f] * (wr * mis[0] + wi * mis[1])
                GS[pl.ds(r, 8), :] = g
        return 0

    for g in range(NGC):
        lax.fori_loop(g * (XL // NGC // UN), (g + 1) * (XL // NGC // UN), outputs, 0)
        grad_copy(g).start()

    for g in range(NGC):
        grad_copy(g).wait_recv()

        def add(i, _):
            for n in range(8):
                o = pl.multiple_of(i * 64, 8) + n * 8
                grad_o[pl.ds(o, 8), :] = GS[pl.ds(o, 8), :] + GR[pl.ds(o, 8), :]
            return 0

        lax.fori_loop(g * GROWS // 64, (g + 1) * GROWS // 64, add, 0)

    for g in range(NGC):
        grad_copy(g).wait_send()
    reduce_drain()


def solution(mesh):
    GX, GY = mesh.shape["gx"], mesh.shape["gy"]

    def on_device(model, freq_sq, source, observed, receiver_depth):
        XL, YL, ZL = model.shape
        PX = XL + 2
        f32 = jnp.float32
        N1, N2 = GX * 2, GY // 2
        NGC = 4
        big = pltpu.VMEM((4, PX * YL, ZL), f32)
        col = pltpu.VMEM((XL * YL, ZL), f32)
        dma = pltpu.SemaphoreType.DMA
        field, grad = pl.pallas_call(
            functools.partial(kernel, (GX, GY, XL, YL, NGC)),
            out_shape=(jax.ShapeDtypeStruct((4, XL * YL, ZL), f32),
                       jax.ShapeDtypeStruct((XL * YL, ZL), f32)),
            in_specs=[pl.BlockSpec(memory_space=pltpu.HBM),
                      pl.BlockSpec(memory_space=pltpu.SMEM),
                      pl.BlockSpec(memory_space=pltpu.HBM),
                      pl.BlockSpec(memory_space=pltpu.HBM),
                      pl.BlockSpec(memory_space=pltpu.HBM)],
            out_specs=(pl.BlockSpec(memory_space=pltpu.VMEM),) * 2,
            scratch_shapes=[
                big, big, big, big,
                pltpu.VMEM((4, XL * YL, ZL), f32),
                col, col,
                pltpu.VMEM((4, XL * YL, ZL), f32),
                pltpu.VMEM((4 * XL, YL), f32),
                pltpu.VMEM((XL, YL), jnp.int32),
                pltpu.VMEM((2, 2, 4, YL + 16, ZL), f32),
                pltpu.VMEM((2, 2, 4, YL, ZL), f32),
                pltpu.VMEM((2, 2, 4, XL + 16, ZL), f32),
                pltpu.VMEM((2, 2, 4, XL, ZL), f32),
                pltpu.VMEM((2, 2, 2, 4, XL, ZL), f32),
                pltpu.VMEM((2, YL, ZL), f32),
                pltpu.VMEM((2, XL, ZL), f32),
                pltpu.VMEM((2, XL, ZL), f32),
                pltpu.VMEM((4, 8, ZL), f32),
                pltpu.VMEM((4, 8, ZL), f32),
                pltpu.VMEM((2, 4, 8, ZL), f32),
                pltpu.VMEM((2, 4, 8, ZL), f32),
                pltpu.VMEM((4, max(XL, YL), ZL), f32),
                pltpu.VMEM((4, 4, max(XL, YL), ZL), f32),
                pltpu.VMEM((4, 4, max(XL, YL), ZL), f32),
                pltpu.VMEM((N1, ZL), f32),
                pltpu.VMEM((N2, ZL), f32),
                col, col,
                dma((7,)), dma((2, 2, 4)), dma((2, 2, 4)), dma((2, 4)), dma((2, 4)), dma((2, 4)), dma((2, 4)),
                dma((N1,)), dma((N1,)), dma((N2,)), dma((N2,)),
                pltpu.SemaphoreType.REGULAR((4, 4)),
                dma((NGC,)), dma((NGC,)),
            ],
            compiler_params=pltpu.CompilerParams(
                collective_id=0, has_side_effects=True, vmem_limit_bytes=26 * 2**20),
        )(*[pltpu.with_memory_space_constraint(a, pltpu.HBM) for a in (
            model.reshape(XL * YL, ZL), freq_sq, source.reshape(4, XL * YL, ZL),
            observed.reshape(4 * XL, YL), receiver_depth)])
        return field.reshape(2, 2, XL, YL, ZL), grad.reshape(XL, YL, ZL)

    in_specs = (
        P("gx", "gy", None),
        P("af"),
        P("af", None, "gx", "gy", None),
        P("af", None, "gx", "gy"),
        P("gx", "gy"),
    )
    out_specs = (P("af", None, "gx", "gy", None), P("gx", "gy", None))
    return jax.shard_map(
        on_device, mesh=mesh, in_specs=in_specs, out_specs=out_specs, check_vma=False
    )
```

```python
import functools

import jax
import jax.numpy as jnp
from jax import lax
from jax.experimental import pallas as pl
from jax.experimental.pallas import tpu as pltpu
from jax.sharding import PartitionSpec as P

MESH = pl.DeviceIdType.MESH
ATTENUATION = 0.2
PENALTY = 4.0


def kernel(dims, model_h, fsq, src_h, obs_h, depth_h, field_o, grad_o,
           S, B, U, Q, PP, M, W, WO, OB, DP, X1, X2, Y1, Y2, YS, MX, MY, MYS, IS, IR, CS, CR, WH, WOH, BH,
           A1R, A2R, GS, GR,
           load_sem, hs_sem, hr_sem, ms_sem, mr_sem, cs_sem, cr_sem,
           a1s_sem, a1r_sem, a2s_sem, a2r_sem, tok_sem, gs_sem, gr_sem):
    GX, GY, XL, YL, NGC = dims
    PX = XL + 2
    NT = YL // 8
    XT = XL // 8
    N1 = GX * 2
    N2 = GY // 2
    gx = lax.axis_index("gx")
    gy = lax.axis_index("gy")
    af = lax.axis_index("af")

    def first(j):
        r = lax.rem(gx * 2 + lax.rem(gy, 2) + j, N1)
        return r // 2, (gy // 2) * 2 + lax.rem(r, 2)

    def second(j):
        return lax.rem(gy // 2 + j, N2) * 2 + lax.rem(gy, 2)

    def axis_peer(n, sign, axis):
        at, size, name = ((gx, GX, "gx"), (gy, GY, "gy"))[axis]
        return (at >= n, {name: at - n}) if sign < 0 else (at < size - n, {name: at + n})

    barrier = pltpu.get_barrier_semaphore()
    pl.semaphore_signal(barrier, inc=1, device_id={"af": 1 - af}, device_id_type=MESH)
    peers = jnp.int32(1)
    for axis in range(2):
        for sign in (-1, 1):
            cond, dev = axis_peer(1, sign, axis)
            peers = peers + cond.astype(jnp.int32)

            @pl.when(cond)
            def _():
                pl.semaphore_signal(barrier, inc=1, device_id=dev, device_id_type=MESH)

    def tell(r, n):
        for axis in range(2):
            for sign in (-1, 1):
                cond, dev = axis_peer(n, sign, axis)

                @pl.when(cond)
                def _():
                    pl.semaphore_signal(tok_sem.at[r, 2 * axis + (sign < 0)], inc=1, device_id=dev,
                                        device_id_type=MESH)

    def told(r, n):
        for axis in range(2):
            for sign in (-1, 1):
                cond, dev = axis_peer(n, sign, axis)

                @pl.when(cond)
                def _():
                    pl.semaphore_wait(tok_sem.at[r, 2 * axis + (sign > 0)], 1)

    loads = [
        pltpu.make_async_copy(depth_h, DP, load_sem.at[4]),
        pltpu.make_async_copy(obs_h, OB, load_sem.at[5]),
        pltpu.make_async_copy(model_h, M, load_sem.at[6]),
    ] + [
        pltpu.make_async_copy(src_h.at[c], S.at[c, pl.ds(YL, XL * YL), :], load_sem.at[c]) for c in range(4)
    ]
    for cp in loads:
        cp.start()

    zero = jnp.zeros((8, 128), jnp.float32)

    for ref in (S, B, U, Q):
        for c in range(4):
            for xx in (0, PX - 1):
                for t in range(NT):
                    ref[c, pl.ds(xx * YL + t * 8, 8), :] = zero

    def clear(ref, side, count):
        for e in range(2):
            for c in range(4):
                for r in range(0, count, 8):
                    ref[e, side, c, pl.ds(8 + r, 8), :] = zero

    has = ((gx > 0, gx < GX - 1), (gy > 0, gy < GY - 1))
    for side in range(2):
        pl.when(jnp.logical_not(has[0][side]))(functools.partial(clear, X1, side, YL))
        pl.when(jnp.logical_not(has[1][side]))(functools.partial(clear, Y1, side, XL))
    for sx in range(2):
        for sy in range(2):
            @pl.when(jnp.logical_not(jnp.logical_and(has[0][sx], has[1][sy])))
            def _():
                for e in range(2):
                    CR[e, 2 * sx + sy] = zero

    for face in range(4):
        @pl.when(jnp.logical_not(has[face // 2][face % 2]))
        def _():
            IR[face] = zero

    def remote(src, dst, ssem, rsem, dev):
        return pltpu.make_async_remote_copy(
            src_ref=src, dst_ref=dst, send_sem=ssem, recv_sem=rsem, device_id=dev, device_id_type=MESH)

    def face_dev(face):
        axis, side = face // 2, face % 2
        step = 2 * side - 1
        return has[axis][side], ({"gx": gx + step} if axis == 0 else {"gy": gy + step})

    def layer_copy(e, l, V, face):
        axis, side = face // 2, face % 2
        there = 1 - side
        if axis == 0:
            plane = l if side == 0 else XL - 1 - l
            src = V.at[:, pl.ds((1 + plane) * YL, YL), :]
            dst = X1.at[e, there, :, pl.ds(8, YL), :] if l == 0 else X2.at[e, there]
        else:
            src = YS.at[e, side, l]
            dst = Y1.at[e, there, :, pl.ds(8, XL), :] if l == 0 else Y2.at[e, there]
        cond, dev = face_dev(face)
        return cond, remote(src, dst, hs_sem.at[e, l, face], hr_sem.at[e, l, 2 * axis + there], dev)

    def model_copy(face):
        axis, side = face // 2, face % 2
        there = 1 - side
        if axis == 0:
            src, dst = M.at[pl.ds(side * (XL - 1) * YL, YL), :], MX.at[there]
        else:
            src, dst = MYS.at[side], MY.at[there]
        cond, dev = face_dev(face)
        return cond, remote(src, dst, ms_sem.at[0, face], mr_sem.at[0, 2 * axis + there], dev)

    def info_copy(face):
        axis, side = face // 2, face % 2
        there = 2 * axis + 1 - side
        cond, dev = face_dev(face)
        return cond, remote(IS.at[face], IR.at[there], ms_sem.at[1, face], mr_sem.at[1, there], dev)

    def corner_copy(e, k):
        sx, sy = k // 2, k % 2
        return jnp.logical_and(has[0][sx], has[1][sy]), remote(
            CS.at[e, k, pl.ds(0, 4), :], CR.at[e, 3 - k, pl.ds(0, 4), :], cs_sem.at[e, k], cr_sem.at[e, 3 - k],
            {"gx": gx + (2 * sx - 1), "gy": gy + (2 * sy - 1)})

    FACES = (0, 1, 2, 3)
    other = lambda face: face ^ 1

    def start_all(copies):
        for cond, cp in copies:
            pl.when(cond)(cp.start)

    def drain_all(copies):
        for cond, cp in copies:
            pl.when(cond)(cp.wait_send)

    def arrive_all(make, faces):
        for face in faces:
            cond, _ = face_dev(face)
            pl.when(cond)(make(other(face))[1].wait_recv)

    def arrive_layer(e, l, V):
        arrive_all(lambda face: layer_copy(e, l, V, face), FACES)

    def arrive_corners(e):
        for k in range(4):
            pl.when(jnp.logical_and(has[0][k // 2], has[1][k % 2]))(corner_copy(e, 3 - k)[1].wait_recv)
        for k in range(4):
            sx, sy = k // 2, k % 2
            for c in range(4):
                v = CR[e, k, pl.ds(c, 1), :]
                X1[e, sx, c, pl.ds(8 + YL if sy else 7, 1), :] = v
                Y1[e, sy, c, pl.ds(8 + XL if sx else 7, 1), :] = v

    def pack_layer(e, l, V):
        for side in range(2):
            y = l if side == 0 else YL - 1 - l
            for c in range(4):
                for k in range(XT):
                    YS[e, side, l, c, pl.ds(k * 8, 8), :] = V[c, pl.ds((1 + 8 * k) * YL + y, 8, stride=YL), :]

    def pack_corners(e, V):
        for k in range(4):
            o = (1 + (XL - 1) * (k // 2)) * YL + (YL - 1) * (k % 2)
            for c in range(4):
                CS[e, k, pl.ds(c, 1), :] = V[c, pl.ds(o, 1), :]

    lane = lax.broadcasted_iota(jnp.int32, (8, 128), 1)
    at_first = lane == 0
    at_last = lane == 127
    sq = [fsq[0], fsq[1]]

    sub = lax.broadcasted_iota(jnp.int32, (8, 128), 0)
    UN = 2

    def around(V, c, o, t):
        cen = V[c, pl.ds(o, 8), :]
        total = V[c, pl.ds(o - YL, 8), :] + V[c, pl.ds(o + YL, 8), :]
        ym, yp = V[c, pl.ds(o - 1, 8), :], V[c, pl.ds(o + 1, 8), :]
        if t == 0:
            ym = jnp.where(sub == 0, 0.0, ym)
        if t == NT - 1:
            yp = jnp.where(sub == 7, 0.0, yp)
        total = total + (ym + yp)
        lo = jnp.where(at_first, 0.0, pltpu.roll(cen, 1, 1))
        hi = jnp.where(at_last, 0.0, pltpu.roll(cen, 127, 1))
        return cen, total + (lo + hi)

    def coefs(f, m, sign):
        k = sq[f] * m
        return 6.0 - k, (sign * ATTENUATION) * k

    def tiles_of(V, sign, finish, r0, tiles, carry):
        for t in tiles:
            m = M[pl.ds(r0 + t * 8, 8), :]
            for f in range(2):
                cr, ci = coefs(f, m, sign)
                o = r0 + YL + t * 8
                re, nre = around(V, 2 * f, o, t)
                im, nim = around(V, 2 * f + 1, o, t)
                out = (cr * re - ci * im - nre, cr * im + ci * re - nim)
                carry = finish(f, o, r0 + t * 8, (re, im), out, carry)
        return carry

    def planes(V, sign, finish, carry, lo, hi, un, tiles):
        def body(i, carry):
            for p in range(un):
                r0 = pl.multiple_of(i * (un * YL), 8) + (lo + p) * YL
                carry = tiles_of(V, sign, finish, r0, tiles, carry)
            return carry
        if not tiles:
            return carry
        return lax.fori_loop(0, (hi - lo) // un, body, carry)

    def sweep(V, sign, finish, carry):
        return planes(V, sign, finish, carry, 0, XL, UN, range(NT))

    def sweep_inner(V, sign, finish, carry):
        return planes(V, sign, finish, carry, 2, XL - 2, 4, range(1, NT - 1))

    def sweep_outer(V, sign, finish, carry):
        carry = planes(V, sign, finish, carry, 2, XL - 2, 4, (0, NT - 1))
        def ends(i, carry):
            for p in range(2):
                r0 = pl.multiple_of(i * ((XL - 2) * YL), 8) + p * YL
                carry = tiles_of(V, sign, finish, r0, range(NT), carry)
            return carry
        return lax.fori_loop(0, 2, ends, carry)

    def strip(e, V, face, finish, carry):
        axis, side = face // 2, face % 2
        H1, H2, MH, L = (X1, X2, MX, YL) if axis == 0 else (Y1, Y2, MY, XL)
        for k in range(L // 8):
            m = MH[side, pl.ds(8 * k, 8), :]
            for f in range(2):
                cr, ci = coefs(f, m, -1.0)
                cen, nb = [], []
                for c in (2 * f, 2 * f + 1):
                    v = H1[e, side, c, pl.ds(8 + 8 * k, 8), :]
                    if axis == 0:
                        inward = V[c, pl.ds((1 + side * (XL - 1)) * YL + 8 * k, 8), :]
                    else:
                        inward = V[c, pl.ds((1 + 8 * k) * YL + side * (YL - 1), 8, stride=YL), :]
                    total = (H2[e, side, c, pl.ds(8 * k, 8), :] + inward) + (
                        H1[e, side, c, pl.ds(7 + 8 * k, 8), :] + H1[e, side, c, pl.ds(9 + 8 * k, 8), :])
                    lo = jnp.where(at_first, 0.0, pltpu.roll(v, 1, 1))
                    hi = jnp.where(at_last, 0.0, pltpu.roll(v, 127, 1))
                    cen.append(v)
                    nb.append(total + (lo + hi))
                out = (cr * cen[0] - ci * cen[1] - nb[0], cr * cen[1] + ci * cen[0] - nb[1])
                carry = finish(face, k, f, out, carry)
        return carry

    def on_face(rows, face, c, k):
        axis, side = face // 2, face % 2
        if axis == 0:
            return rows(c, 1 + side * (XL - 1), 8 * k, False)
        return rows(c, 1 + 8 * k, side * (YL - 1), True)

    def take(ref, idx, h, f, carry):
        old = ref[idx[0], idx[1], :]
        ref[idx[0], idx[1], :] = old - h
        d = h * (h - 2.0 * old)
        return tuple(carry[i] + d if i == f else carry[i] for i in range(2))

    def correct(e, ref, carry):
        for face in range(4):
            H1, L = (X1, YL) if face < 2 else (Y1, XL)
            for c in range(4):
                for k in range(L // 8):
                    h = H1[e, face % 2, c, pl.ds(8 + 8 * k, 8), :]
                    carry = take(ref, on_face(padded, face, c, k), h, c // 2, carry)
        return carry

    def padded(c, xx, yy, strided):
        o = xx * YL + yy
        return c, pl.ds(o, 8, stride=YL) if strided else pl.ds(o, 8)

    def compact(c, xx, yy, strided):
        return padded(c, xx - 1, yy, strided)

    for cp in loads[3:]:
        cp.wait()
    pl.semaphore_wait(barrier, peers)
    start_all([layer_copy(0, l, S, face) for l in range(2) for face in (0, 1)])
    tell(0, 1)
    for l in range(2):
        pack_layer(0, l, S)
        start_all([layer_copy(0, l, S, face) for face in (2, 3)])
    pack_corners(0, S)
    loads[0].wait()
    loads[1].wait()
    dt = jnp.transpose(jnp.concatenate(
        [DP[...].astype(jnp.float32), jnp.zeros((XL, 128 - YL), jnp.float32)], axis=1))
    ot = jnp.transpose(jnp.concatenate(
        [OB[...], jnp.zeros((4 * XL, 128 - YL), jnp.float32)], axis=1))
    for face in range(4):
        IS[face] = zero
    for side in range(2):
        x, y = side * (XL - 1), side * (YL - 1)
        for c in range(4):
            IS[side, c:c + 1, 0:YL] = OB[c * XL + x:c * XL + x + 1, :]
        IS[side, 4:5, 0:YL] = DP[x:x + 1, :].astype(jnp.float32)
        IS[2 + side, 0:1, 0:4 * XL] = ot[y:y + 1, :]
        IS[2 + side, 1:2, 0:XL] = dt[y:y + 1, :]
    loads[2].wait()
    for side in range(2):
        for k in range(XT):
            MYS[side, pl.ds(8 * k, 8), :] = M[pl.ds(8 * k * YL + side * (YL - 1), 8, stride=YL), :]
    start_all([info_copy(face) for face in FACES])
    start_all([model_copy(face) for face in FACES])

    lanef = lane.astype(jnp.float32)
    for x in range(XL):
        for t in range(NT):
            d = jnp.broadcast_to(dt[t * 8:t * 8 + 8, x:x + 1], (8, 128))
            w = jnp.where(lanef == d, PENALTY, 0.0)
            W[pl.ds(x * YL + t * 8, 8), :] = w
            for c in range(4):
                ob = jnp.broadcast_to(ot[t * 8:t * 8 + 8, c * XL + x:c * XL + x + 1], (8, 128))
                WO[c, pl.ds(x * YL + t * 8, 8), :] = w * ob

    def finish_b(f, o, r, cen, out, carry):
        acc = carry[f]
        for c in range(2):
            v = out[c] + WO[2 * f + c, pl.ds(r, 8), :]
            B[2 * f + c, pl.ds(o, 8), :] = v
            acc = acc + v * v
        return tuple(acc if i == f else carry[i] for i in range(2))

    told(0, 1)
    start_all([corner_copy(0, k) for k in range(4)])
    tell(1, 2)
    rr = sweep(S, -1.0, finish_b, (zero, zero))

    def finish_u(f, o, r, cen, out, carry):
        acc = carry[f]
        for c in range(2):
            U[2 * f + c, pl.ds(o, 8), :] = out[c]
            acc = acc + out[c] * out[c]
        return tuple(acc if i == f else carry[i] for i in range(2))

    dq = sweep_inner(B, 1.0, finish_u, (zero, zero))
    arrive_layer(0, 0, S)
    rr = correct(0, B, rr)
    told(1, 2)
    tell(2, 4)
    dq = sweep_outer(B, 1.0, finish_u, dq)

    arrive_all(info_copy, FACES)
    it = jnp.transpose(jnp.concatenate(
        [IR[face] for face in range(4)] + [jnp.zeros((96, 128), jnp.float32)], axis=0))
    for face in range(4):
        L = YL if face < 2 else XL
        for k in range(L // 8):
            if face < 2:
                d = it[8 * k:8 * k + 8, 8 * face + 4:8 * face + 5]
                obs = [it[8 * k:8 * k + 8, 8 * face + c:8 * face + c + 1] for c in range(4)]
            else:
                d = it[8 * k:8 * k + 8, 8 * face + 1:8 * face + 2]
                obs = [it[c * XL + 8 * k:c * XL + 8 * k + 8, 8 * face:8 * face + 1] for c in range(4)]
            w = jnp.where(lanef == jnp.broadcast_to(d, (8, 128)), PENALTY, 0.0)
            WH[face, pl.ds(8 * k, 8), :] = w
            for c in range(4):
                WOH[face, c, pl.ds(8 * k, 8), :] = w * jnp.broadcast_to(obs[c], (8, 128))

    def finish_bh(face, k, f, out, carry):
        cond, _ = face_dev(face)
        for i in range(2):
            c = 2 * f + i
            v = jnp.where(cond, out[i] + WOH[face, c, pl.ds(8 * k, 8), :], 0.0)
            BH[face, c, pl.ds(8 * k, 8), :] = v
            carry = take(U, on_face(padded, face, c, k), v, f, carry)
        return carry

    arrive_all(model_copy, FACES)
    arrive_layer(0, 1, S)
    arrive_corners(0)
    for face in FACES:
        dq = strip(0, S, face, finish_bh, dq)
    pack_corners(1, U)
    start_all([corner_copy(1, k) for k in range(4)])
    start_all([layer_copy(1, l, U, face) for l in range(2) for face in (0, 1)])
    for l in range(2):
        pack_layer(1, l, U)
        start_all([layer_copy(1, l, U, face) for face in (2, 3)])
    told(2, 4)
    tell(3, 8)

    def finish_q(f, o, r, cen, out, carry):
        dq, qq = carry[f], carry[2 + f]
        w = W[pl.ds(r, 8), :]
        for c in range(2):
            b = B[2 * f + c, pl.ds(o, 8), :]
            wb = w * b
            v = out[c] + wb
            Q[2 * f + c, pl.ds(o, 8), :] = v
            dq = dq + wb * b
            qq = qq + v * v
        carry = list(carry)
        carry[f], carry[2 + f] = dq, qq
        return tuple(carry)

    carry = sweep(U, -1.0, finish_q, tuple(dq) + (zero, zero))
    dq, qq = carry[:2], carry[2:]
    def finish_p(f, o, r, cen, out, carry):
        acc = carry[f]
        w = W[pl.ds(r, 8), :]
        for c in range(2):
            PP[2 * f + c, pl.ds(r, 8), :] = out[c]
            acc = acc + (out[c] * out[c] + w * (cen[c] * cen[c]))
        return tuple(acc if i == f else carry[i] for i in range(2))

    qmq = sweep_inner(Q, 1.0, finish_p, (zero, zero))
    arrive_layer(1, 0, U)
    qq = correct(1, Q, qq)
    told(3, 8)
    qmq = sweep_outer(Q, 1.0, finish_p, qmq)

    def finish_qh(face, k, f, out, carry):
        cond, _ = face_dev(face)
        w = WH[face, pl.ds(8 * k, 8), :]
        for i in range(2):
            c = 2 * f + i
            v = jnp.where(cond, out[i] + w * BH[face, c, pl.ds(8 * k, 8), :], 0.0)
            carry = take(PP, on_face(compact, face, c, k), v, f, carry)
        return carry

    arrive_layer(1, 1, U)
    arrive_corners(1)
    for face in FACES:
        qmq = strip(1, U, face, finish_qh, qmq)

    group = lane // 16

    def first_copy(j, slot):
        px, py = first(j)
        return pltpu.make_async_remote_copy(
            src_ref=A1R.at[pl.ds(0, 1), :], dst_ref=A1R.at[pl.ds(slot, 1), :],
            send_sem=a1s_sem.at[j], recv_sem=a1r_sem.at[slot],
            device_id={"gx": px, "gy": py}, device_id_type=MESH)

    def second_copy(j, slot):
        return pltpu.make_async_remote_copy(
            src_ref=A2R.at[pl.ds(0, 1), :], dst_ref=A2R.at[pl.ds(slot, 1), :],
            send_sem=a2s_sem.at[j], recv_sem=a2r_sem.at[slot],
            device_id={"gy": second(j)}, device_id_type=MESH)

    def reduce_first(parts):
        mix = zero
        for i, v in enumerate(parts):
            for shift in (64, 32, 16):
                v = v + pltpu.roll(v, shift, 1)
            mix = jnp.where(group == i, v, mix)
        A1R[pl.ds(0, 1), :] = jnp.sum(mix, axis=0, keepdims=True)
        for j in range(1, N1):
            first_copy(j, N1 - j).start()

    def reduce_second():
        for j in range(1, N1):
            first_copy(j, j).wait_recv()
        A2R[pl.ds(0, 1), :] = jnp.sum(A1R[...], axis=0, keepdims=True)
        for j in range(1, N2):
            second_copy(j, N2 - j).start()

    def reduce_end():
        for j in range(1, N2):
            second_copy(j, j).wait_recv()
        v = jnp.broadcast_to(jnp.sum(A2R[...], axis=0, keepdims=True), (8, 128))
        for shift in (8, 4, 2, 1):
            v = v + pltpu.roll(v, 128 - shift, 1)
        return v

    def reduce_drain():
        for j in range(1, N1):
            first_copy(j, j).wait_send()
        for j in range(1, N2):
            second_copy(j, j).wait_send()

    def row(sums, i):
        return jnp.broadcast_to(sums[:, 16 * i:16 * i + 1], (8, 128))

    reduce_first((rr[0], rr[1], dq[0], dq[1], qq[0], qq[1], qmq[0], qmq[1]))
    for e, V in ((0, S), (1, U)):
        for l in range(2):
            drain_all([layer_copy(e, l, V, face) for face in FACES])
        drain_all([corner_copy(e, k) for k in range(4)])
    drain_all([model_copy(face) for face in FACES])
    drain_all([info_copy(face) for face in FACES])
    reduce_second()
    sums = reduce_end()

    cb, cq = [], []
    for f in range(2):
        norm0, curv0, qq0, qmq0 = (row(sums, 2 * i + f) for i in range(4))
        alpha0 = norm0 / curv0
        norm1 = norm0 - alpha0 * (2.0 * curv0 - alpha0 * qq0)
        beta = norm1 / norm0
        rq = curv0 - alpha0 * qq0
        rmr = curv0 - alpha0 * (2.0 * qq0 - alpha0 * qmq0)
        alpha1 = norm1 / (rmr + beta * (2.0 * rq + beta * curv0))
        cb.append(alpha0 + alpha1 * (1.0 + beta))
        cq.append(-(alpha0 * alpha1))

    GROWS = XL * YL // NGC
    def grad_copy(g):
        return pltpu.make_async_remote_copy(
            src_ref=GS.at[pl.ds(g * GROWS, GROWS), :], dst_ref=GR.at[pl.ds(g * GROWS, GROWS), :],
            send_sem=gs_sem.at[g], recv_sem=gr_sem.at[g], device_id={"af": 1 - af}, device_id_type=MESH)

    def outputs(i, _):
        for p in range(UN):
            r0 = pl.multiple_of(i * (UN * YL), 8) + p * YL
            for t in range(NT):
                r = r0 + t * 8
                g = zero
                for f in range(2):
                    fld, mis = [], []
                    for c in range(2):
                        n = 2 * f + c
                        v = cb[f] * B[n, pl.ds(r + YL, 8), :] + cq[f] * Q[n, pl.ds(r + YL, 8), :]
                        field_o[n, pl.ds(r, 8), :] = v
                        fld.append(v)
                        mis.append(cb[f] * U[n, pl.ds(r + YL, 8), :] + cq[f] * PP[n, pl.ds(r, 8), :]
                                   - S[n, pl.ds(r + YL, 8), :])
                    wr = -fld[0] - ATTENUATION * fld[1]
                    wi = ATTENUATION * fld[0] - fld[1]
                    g = g + sq[f] * (wr * mis[0] + wi * mis[1])
                GS[pl.ds(r, 8), :] = g
        return 0

    for g in range(NGC):
        lax.fori_loop(g * (XL // NGC // UN), (g + 1) * (XL // NGC // UN), outputs, 0)
        grad_copy(g).start()

    for g in range(NGC):
        grad_copy(g).wait_recv()

        def add(i, _):
            for n in range(8):
                o = pl.multiple_of(i * 64, 8) + n * 8
                grad_o[pl.ds(o, 8), :] = GS[pl.ds(o, 8), :] + GR[pl.ds(o, 8), :]
            return 0

        lax.fori_loop(g * GROWS // 64, (g + 1) * GROWS // 64, add, 0)

    for g in range(NGC):
        grad_copy(g).wait_send()
    reduce_drain()


def solution(mesh):
    GX, GY = mesh.shape["gx"], mesh.shape["gy"]

    def on_device(model, freq_sq, source, observed, receiver_depth):
        XL, YL, ZL = model.shape
        PX = XL + 2
        f32 = jnp.float32
        N1, N2 = GX * 2, GY // 2
        NGC = 4
        big = pltpu.VMEM((4, PX * YL, ZL), f32)
        col = pltpu.VMEM((XL * YL, ZL), f32)
        dma = pltpu.SemaphoreType.DMA
        field, grad = pl.pallas_call(
            functools.partial(kernel, (GX, GY, XL, YL, NGC)),
            out_shape=(jax.ShapeDtypeStruct((4, XL * YL, ZL), f32),
                       jax.ShapeDtypeStruct((XL * YL, ZL), f32)),
            in_specs=[pl.BlockSpec(memory_space=pltpu.HBM),
                      pl.BlockSpec(memory_space=pltpu.SMEM),
                      pl.BlockSpec(memory_space=pltpu.HBM),
                      pl.BlockSpec(memory_space=pltpu.HBM),
                      pl.BlockSpec(memory_space=pltpu.HBM)],
            out_specs=(pl.BlockSpec(memory_space=pltpu.VMEM),) * 2,
            scratch_shapes=[
                big, big, big, big,
                pltpu.VMEM((4, XL * YL, ZL), f32),
                col, col,
                pltpu.VMEM((4, XL * YL, ZL), f32),
                pltpu.VMEM((4 * XL, YL), f32),
                pltpu.VMEM((XL, YL), jnp.int32),
                pltpu.VMEM((2, 2, 4, YL + 16, ZL), f32),
                pltpu.VMEM((2, 2, 4, YL, ZL), f32),
                pltpu.VMEM((2, 2, 4, XL + 16, ZL), f32),
                pltpu.VMEM((2, 2, 4, XL, ZL), f32),
                pltpu.VMEM((2, 2, 2, 4, XL, ZL), f32),
                pltpu.VMEM((2, YL, ZL), f32),
                pltpu.VMEM((2, XL, ZL), f32),
                pltpu.VMEM((2, XL, ZL), f32),
                pltpu.VMEM((4, 8, ZL), f32),
                pltpu.VMEM((4, 8, ZL), f32),
                pltpu.VMEM((2, 4, 8, ZL), f32),
                pltpu.VMEM((2, 4, 8, ZL), f32),
                pltpu.VMEM((4, max(XL, YL), ZL), f32),
                pltpu.VMEM((4, 4, max(XL, YL), ZL), f32),
                pltpu.VMEM((4, 4, max(XL, YL), ZL), f32),
                pltpu.VMEM((N1, ZL), f32),
                pltpu.VMEM((N2, ZL), f32),
                col, col,
                dma((7,)), dma((2, 2, 4)), dma((2, 2, 4)), dma((2, 4)), dma((2, 4)), dma((2, 4)), dma((2, 4)),
                dma((N1,)), dma((N1,)), dma((N2,)), dma((N2,)),
                pltpu.SemaphoreType.REGULAR((4, 4)),
                dma((NGC,)), dma((NGC,)),
            ],
            compiler_params=pltpu.CompilerParams(
                collective_id=0, has_side_effects=True, vmem_limit_bytes=26 * 2**20),
        )(*[pltpu.with_memory_space_constraint(a, pltpu.HBM) for a in (
            model.reshape(XL * YL, ZL), freq_sq, source.reshape(4, XL * YL, ZL),
            observed.reshape(4 * XL, YL), receiver_depth)])
        return field.reshape(2, 2, XL, YL, ZL), grad.reshape(XL, YL, ZL)

    in_specs = (
        P("gx", "gy", None),
        P("af"),
        P("af", None, "gx", "gy", None),
        P("af", None, "gx", "gy"),
        P("gx", "gy"),
    )
    out_specs = (P("af", None, "gx", "gy", None), P("gx", "gy", None))
    return jax.shard_map(
        on_device, mesh=mesh, in_specs=in_specs, out_specs=out_specs, check_vma=False
    )
```

```python
import functools

import jax
import jax.numpy as jnp
from jax import lax
from jax.experimental import pallas as pl
from jax.experimental.pallas import tpu as pltpu
from jax.sharding import PartitionSpec as P

MESH = pl.DeviceIdType.MESH
ATTENUATION = 0.2
PENALTY = 4.0


def kernel(dims, model_h, fsq, src_h, obs_h, depth_h, field_o, grad_o,
           S, B, U, Q, PP, M, W, WO, OB, DP, X1, X2, Y1, Y2, YS, MX, MY, MYS, IS, IR, CS, CR, WH, WOH, BH,
           A1R, GS, GR,
           load_sem, hs_sem, hr_sem, ms_sem, mr_sem, cs_sem, cr_sem,
           a1s_sem, a1r_sem, tok_sem, gs_sem, gr_sem):
    GX, GY, XL, YL, NGC = dims
    PX = XL + 2
    NT = YL // 8
    XT = XL // 8
    gx = lax.axis_index("gx")
    gy = lax.axis_index("gy")
    af = lax.axis_index("af")

    def axis_peer(n, sign, axis):
        at, size, name = ((gx, GX, "gx"), (gy, GY, "gy"))[axis]
        return (at >= n, {name: at - n}) if sign < 0 else (at < size - n, {name: at + n})

    barrier = pltpu.get_barrier_semaphore()
    pl.semaphore_signal(barrier, inc=1, device_id={"af": 1 - af}, device_id_type=MESH)
    peers = jnp.int32(1)
    for axis in range(2):
        for sign in (-1, 1):
            cond, dev = axis_peer(1, sign, axis)
            peers = peers + cond.astype(jnp.int32)

            @pl.when(cond)
            def _():
                pl.semaphore_signal(barrier, inc=1, device_id=dev, device_id_type=MESH)

    def tell(r, n):
        for axis in range(2):
            for sign in (-1, 1):
                cond, dev = axis_peer(n, sign, axis)

                @pl.when(cond)
                def _():
                    pl.semaphore_signal(tok_sem.at[r, 2 * axis + (sign < 0)], inc=1, device_id=dev,
                                        device_id_type=MESH)

    def told(r, n):
        for axis in range(2):
            for sign in (-1, 1):
                cond, dev = axis_peer(n, sign, axis)

                @pl.when(cond)
                def _():
                    pl.semaphore_wait(tok_sem.at[r, 2 * axis + (sign > 0)], 1)

    loads = [
        pltpu.make_async_copy(depth_h, DP, load_sem.at[4]),
        pltpu.make_async_copy(obs_h, OB, load_sem.at[5]),
        pltpu.make_async_copy(model_h, M, load_sem.at[6]),
    ] + [
        pltpu.make_async_copy(src_h.at[c], S.at[c, pl.ds(YL, XL * YL), :], load_sem.at[c]) for c in range(4)
    ]
    for cp in loads:
        cp.start()

    zero = jnp.zeros((8, 128), jnp.float32)

    for ref in (S, B, U, Q):
        for c in range(4):
            for xx in (0, PX - 1):
                for t in range(NT):
                    ref[c, pl.ds(xx * YL + t * 8, 8), :] = zero

    def clear(ref, side, count):
        for e in range(2):
            for c in range(4):
                for r in range(0, count, 8):
                    ref[e, side, c, pl.ds(8 + r, 8), :] = zero

    has = ((gx > 0, gx < GX - 1), (gy > 0, gy < GY - 1))
    for side in range(2):
        pl.when(jnp.logical_not(has[0][side]))(functools.partial(clear, X1, side, YL))
        pl.when(jnp.logical_not(has[1][side]))(functools.partial(clear, Y1, side, XL))
    for sx in range(2):
        for sy in range(2):
            @pl.when(jnp.logical_not(jnp.logical_and(has[0][sx], has[1][sy])))
            def _():
                for e in range(2):
                    CR[e, 2 * sx + sy] = zero

    for face in range(4):
        @pl.when(jnp.logical_not(has[face // 2][face % 2]))
        def _():
            IR[face] = zero

    def remote(src, dst, ssem, rsem, dev):
        return pltpu.make_async_remote_copy(
            src_ref=src, dst_ref=dst, send_sem=ssem, recv_sem=rsem, device_id=dev, device_id_type=MESH)

    def face_dev(face):
        axis, side = face // 2, face % 2
        step = 2 * side - 1
        return has[axis][side], ({"gx": gx + step} if axis == 0 else {"gy": gy + step})

    def layer_copy(e, l, V, face):
        axis, side = face // 2, face % 2
        there = 1 - side
        if axis == 0:
            plane = l if side == 0 else XL - 1 - l
            src = V.at[:, pl.ds((1 + plane) * YL, YL), :]
            dst = X1.at[e, there, :, pl.ds(8, YL), :] if l == 0 else X2.at[e, there]
        else:
            src = YS.at[e, side, l]
            dst = Y1.at[e, there, :, pl.ds(8, XL), :] if l == 0 else Y2.at[e, there]
        cond, dev = face_dev(face)
        return cond, remote(src, dst, hs_sem.at[e, l, face], hr_sem.at[e, l, 2 * axis + there], dev)

    def model_copy(face):
        axis, side = face // 2, face % 2
        there = 1 - side
        if axis == 0:
            src, dst = M.at[pl.ds(side * (XL - 1) * YL, YL), :], MX.at[there]
        else:
            src, dst = MYS.at[side], MY.at[there]
        cond, dev = face_dev(face)
        return cond, remote(src, dst, ms_sem.at[0, face], mr_sem.at[0, 2 * axis + there], dev)

    def info_copy(face):
        axis, side = face // 2, face % 2
        there = 2 * axis + 1 - side
        cond, dev = face_dev(face)
        return cond, remote(IS.at[face], IR.at[there], ms_sem.at[1, face], mr_sem.at[1, there], dev)

    def corner_copy(e, k):
        sx, sy = k // 2, k % 2
        return jnp.logical_and(has[0][sx], has[1][sy]), remote(
            CS.at[e, k, pl.ds(0, 4), :], CR.at[e, 3 - k, pl.ds(0, 4), :], cs_sem.at[e, k], cr_sem.at[e, 3 - k],
            {"gx": gx + (2 * sx - 1), "gy": gy + (2 * sy - 1)})

    FACES = (0, 1, 2, 3)
    other = lambda face: face ^ 1

    def start_all(copies):
        for cond, cp in copies:
            pl.when(cond)(cp.start)

    def drain_all(copies):
        for cond, cp in copies:
            pl.when(cond)(cp.wait_send)

    def arrive_all(make, faces):
        for face in faces:
            cond, _ = face_dev(face)
            pl.when(cond)(make(other(face))[1].wait_recv)

    def arrive_layer(e, l, V):
        arrive_all(lambda face: layer_copy(e, l, V, face), FACES)

    def arrive_corners(e):
        for k in range(4):
            pl.when(jnp.logical_and(has[0][k // 2], has[1][k % 2]))(corner_copy(e, 3 - k)[1].wait_recv)
        for k in range(4):
            sx, sy = k // 2, k % 2
            for c in range(4):
                v = CR[e, k, pl.ds(c, 1), :]
                X1[e, sx, c, pl.ds(8 + YL if sy else 7, 1), :] = v
                Y1[e, sy, c, pl.ds(8 + XL if sx else 7, 1), :] = v

    def pack_layer(e, l, V):
        for side in range(2):
            y = l if side == 0 else YL - 1 - l
            for c in range(4):
                for k in range(XT):
                    YS[e, side, l, c, pl.ds(k * 8, 8), :] = V[c, pl.ds((1 + 8 * k) * YL + y, 8, stride=YL), :]

    def pack_corners(e, V):
        for k in range(4):
            o = (1 + (XL - 1) * (k // 2)) * YL + (YL - 1) * (k % 2)
            for c in range(4):
                CS[e, k, pl.ds(c, 1), :] = V[c, pl.ds(o, 1), :]

    lane = lax.broadcasted_iota(jnp.int32, (8, 128), 1)
    at_first = lane == 0
    at_last = lane == 127
    sq = [fsq[0], fsq[1]]

    sub = lax.broadcasted_iota(jnp.int32, (8, 128), 0)
    UN = 2

    def around(V, c, o, t):
        cen = V[c, pl.ds(o, 8), :]
        total = V[c, pl.ds(o - YL, 8), :] + V[c, pl.ds(o + YL, 8), :]
        ym, yp = V[c, pl.ds(o - 1, 8), :], V[c, pl.ds(o + 1, 8), :]
        if t == 0:
            ym = jnp.where(sub == 0, 0.0, ym)
        if t == NT - 1:
            yp = jnp.where(sub == 7, 0.0, yp)
        total = total + (ym + yp)
        lo = jnp.where(at_first, 0.0, pltpu.roll(cen, 1, 1))
        hi = jnp.where(at_last, 0.0, pltpu.roll(cen, 127, 1))
        return cen, total + (lo + hi)

    def coefs(f, m, sign):
        k = sq[f] * m
        return 6.0 - k, (sign * ATTENUATION) * k

    def tiles_of(V, sign, finish, r0, tiles, carry):
        for t in tiles:
            m = M[pl.ds(r0 + t * 8, 8), :]
            for f in range(2):
                cr, ci = coefs(f, m, sign)
                o = r0 + YL + t * 8
                re, nre = around(V, 2 * f, o, t)
                im, nim = around(V, 2 * f + 1, o, t)
                out = (cr * re - ci * im - nre, cr * im + ci * re - nim)
                carry = finish(f, o, r0 + t * 8, (re, im), out, carry)
        return carry

    def planes(V, sign, finish, carry, lo, hi, un, tiles):
        def body(i, carry):
            for p in range(un):
                r0 = pl.multiple_of(i * (un * YL), 8) + (lo + p) * YL
                carry = tiles_of(V, sign, finish, r0, tiles, carry)
            return carry
        if not tiles:
            return carry
        return lax.fori_loop(0, (hi - lo) // un, body, carry)

    def sweep(V, sign, finish, carry):
        return planes(V, sign, finish, carry, 0, XL, UN, range(NT))

    def sweep_inner(V, sign, finish, carry):
        return planes(V, sign, finish, carry, 2, XL - 2, 4, range(1, NT - 1))

    def sweep_outer(V, sign, finish, carry):
        carry = planes(V, sign, finish, carry, 2, XL - 2, 4, (0, NT - 1))
        def ends(i, carry):
            for p in range(2):
                r0 = pl.multiple_of(i * ((XL - 2) * YL), 8) + p * YL
                carry = tiles_of(V, sign, finish, r0, range(NT), carry)
            return carry
        return lax.fori_loop(0, 2, ends, carry)

    def strip(e, V, face, finish, carry):
        axis, side = face // 2, face % 2
        H1, H2, MH, L = (X1, X2, MX, YL) if axis == 0 else (Y1, Y2, MY, XL)
        for k in range(L // 8):
            m = MH[side, pl.ds(8 * k, 8), :]
            for f in range(2):
                cr, ci = coefs(f, m, -1.0)
                cen, nb = [], []
                for c in (2 * f, 2 * f + 1):
                    v = H1[e, side, c, pl.ds(8 + 8 * k, 8), :]
                    if axis == 0:
                        inward = V[c, pl.ds((1 + side * (XL - 1)) * YL + 8 * k, 8), :]
                    else:
                        inward = V[c, pl.ds((1 + 8 * k) * YL + side * (YL - 1), 8, stride=YL), :]
                    total = (H2[e, side, c, pl.ds(8 * k, 8), :] + inward) + (
                        H1[e, side, c, pl.ds(7 + 8 * k, 8), :] + H1[e, side, c, pl.ds(9 + 8 * k, 8), :])
                    lo = jnp.where(at_first, 0.0, pltpu.roll(v, 1, 1))
                    hi = jnp.where(at_last, 0.0, pltpu.roll(v, 127, 1))
                    cen.append(v)
                    nb.append(total + (lo + hi))
                out = (cr * cen[0] - ci * cen[1] - nb[0], cr * cen[1] + ci * cen[0] - nb[1])
                carry = finish(face, k, f, out, carry)
        return carry

    def on_face(rows, face, c, k):
        axis, side = face // 2, face % 2
        if axis == 0:
            return rows(c, 1 + side * (XL - 1), 8 * k, False)
        return rows(c, 1 + 8 * k, side * (YL - 1), True)

    def take(ref, idx, h, f, carry):
        old = ref[idx[0], idx[1], :]
        ref[idx[0], idx[1], :] = old - h
        d = h * (h - 2.0 * old)
        return tuple(carry[i] + d if i == f else carry[i] for i in range(2))

    def correct(e, ref, carry):
        for face in range(4):
            H1, L = (X1, YL) if face < 2 else (Y1, XL)
            for c in range(4):
                for k in range(L // 8):
                    h = H1[e, face % 2, c, pl.ds(8 + 8 * k, 8), :]
                    carry = take(ref, on_face(padded, face, c, k), h, c // 2, carry)
        return carry

    def padded(c, xx, yy, strided):
        o = xx * YL + yy
        return c, pl.ds(o, 8, stride=YL) if strided else pl.ds(o, 8)

    def compact(c, xx, yy, strided):
        return padded(c, xx - 1, yy, strided)

    for cp in loads[3:]:
        cp.wait()
    pl.semaphore_wait(barrier, peers)
    start_all([layer_copy(0, l, S, face) for l in range(2) for face in (0, 1)])
    tell(0, 1)
    for l in range(2):
        pack_layer(0, l, S)
        start_all([layer_copy(0, l, S, face) for face in (2, 3)])
    pack_corners(0, S)
    loads[0].wait()
    loads[1].wait()
    dt = jnp.transpose(jnp.concatenate(
        [DP[...].astype(jnp.float32), jnp.zeros((XL, 128 - YL), jnp.float32)], axis=1))
    ot = jnp.transpose(jnp.concatenate(
        [OB[...], jnp.zeros((4 * XL, 128 - YL), jnp.float32)], axis=1))
    for face in range(4):
        IS[face] = zero
    for side in range(2):
        x, y = side * (XL - 1), side * (YL - 1)
        for c in range(4):
            IS[side, c:c + 1, 0:YL] = OB[c * XL + x:c * XL + x + 1, :]
        IS[side, 4:5, 0:YL] = DP[x:x + 1, :].astype(jnp.float32)
        IS[2 + side, 0:1, 0:4 * XL] = ot[y:y + 1, :]
        IS[2 + side, 1:2, 0:XL] = dt[y:y + 1, :]
    loads[2].wait()
    for side in range(2):
        for k in range(XT):
            MYS[side, pl.ds(8 * k, 8), :] = M[pl.ds(8 * k * YL + side * (YL - 1), 8, stride=YL), :]
    start_all([info_copy(face) for face in FACES])
    start_all([model_copy(face) for face in FACES])

    lanef = lane.astype(jnp.float32)
    for x in range(XL):
        for t in range(NT):
            d = jnp.broadcast_to(dt[t * 8:t * 8 + 8, x:x + 1], (8, 128))
            w = jnp.where(lanef == d, PENALTY, 0.0)
            W[pl.ds(x * YL + t * 8, 8), :] = w
            for c in range(4):
                ob = jnp.broadcast_to(ot[t * 8:t * 8 + 8, c * XL + x:c * XL + x + 1], (8, 128))
                WO[c, pl.ds(x * YL + t * 8, 8), :] = w * ob

    def finish_b(f, o, r, cen, out, carry):
        acc = carry[f]
        for c in range(2):
            v = out[c] + WO[2 * f + c, pl.ds(r, 8), :]
            B[2 * f + c, pl.ds(o, 8), :] = v
            acc = acc + v * v
        return tuple(acc if i == f else carry[i] for i in range(2))

    told(0, 1)
    start_all([corner_copy(0, k) for k in range(4)])
    tell(1, 2)
    rr = sweep(S, -1.0, finish_b, (zero, zero))
    told(1, 2)
    tell(2, 4)

    def finish_u(f, o, r, cen, out, carry):
        acc = carry[f]
        for c in range(2):
            U[2 * f + c, pl.ds(o, 8), :] = out[c]
            acc = acc + out[c] * out[c]
        return tuple(acc if i == f else carry[i] for i in range(2))

    dq = sweep_inner(B, 1.0, finish_u, (zero, zero))
    arrive_layer(0, 0, S)
    rr = correct(0, B, rr)
    told(2, 4)
    tell(3, 8)
    dq = sweep_outer(B, 1.0, finish_u, dq)

    arrive_all(info_copy, FACES)
    it = jnp.transpose(jnp.concatenate(
        [IR[face] for face in range(4)] + [jnp.zeros((96, 128), jnp.float32)], axis=0))
    for face in range(4):
        L = YL if face < 2 else XL
        for k in range(L // 8):
            if face < 2:
                d = it[8 * k:8 * k + 8, 8 * face + 4:8 * face + 5]
                obs = [it[8 * k:8 * k + 8, 8 * face + c:8 * face + c + 1] for c in range(4)]
            else:
                d = it[8 * k:8 * k + 8, 8 * face + 1:8 * face + 2]
                obs = [it[c * XL + 8 * k:c * XL + 8 * k + 8, 8 * face:8 * face + 1] for c in range(4)]
            w = jnp.where(lanef == jnp.broadcast_to(d, (8, 128)), PENALTY, 0.0)
            WH[face, pl.ds(8 * k, 8), :] = w
            for c in range(4):
                WOH[face, c, pl.ds(8 * k, 8), :] = w * jnp.broadcast_to(obs[c], (8, 128))

    def finish_bh(face, k, f, out, carry):
        cond, _ = face_dev(face)
        for i in range(2):
            c = 2 * f + i
            v = jnp.where(cond, out[i] + WOH[face, c, pl.ds(8 * k, 8), :], 0.0)
            BH[face, c, pl.ds(8 * k, 8), :] = v
            carry = take(U, on_face(padded, face, c, k), v, f, carry)
        return carry

    arrive_all(model_copy, FACES)
    arrive_layer(0, 1, S)
    arrive_corners(0)
    for face in FACES:
        dq = strip(0, S, face, finish_bh, dq)
    pack_corners(1, U)
    start_all([corner_copy(1, k) for k in range(4)])
    start_all([layer_copy(1, l, U, face) for l in range(2) for face in (0, 1)])
    for l in range(2):
        pack_layer(1, l, U)
        start_all([layer_copy(1, l, U, face) for face in (2, 3)])
    told(3, 8)
    tell(4, 1)
    tell(5, 4)

    def finish_q(f, o, r, cen, out, carry):
        dq, qq = carry[f], carry[2 + f]
        w = W[pl.ds(r, 8), :]
        for c in range(2):
            b = B[2 * f + c, pl.ds(o, 8), :]
            wb = w * b
            v = out[c] + wb
            Q[2 * f + c, pl.ds(o, 8), :] = v
            dq = dq + wb * b
            qq = qq + v * v
        carry = list(carry)
        carry[f], carry[2 + f] = dq, qq
        return tuple(carry)

    carry = sweep(U, -1.0, finish_q, tuple(dq) + (zero, zero))
    dq, qq = carry[:2], carry[2:]
    def finish_p(f, o, r, cen, out, carry):
        acc = carry[f]
        w = W[pl.ds(r, 8), :]
        for c in range(2):
            PP[2 * f + c, pl.ds(r, 8), :] = out[c]
            acc = acc + (out[c] * out[c] + w * (cen[c] * cen[c]))
        return tuple(acc if i == f else carry[i] for i in range(2))

    told(4, 1)
    told(5, 4)
    tell(6, 2)
    tell(7, 8)
    qmq = sweep_inner(Q, 1.0, finish_p, (zero, zero))
    arrive_layer(1, 0, U)
    qq = correct(1, Q, qq)
    qmq = sweep_outer(Q, 1.0, finish_p, qmq)

    def finish_qh(face, k, f, out, carry):
        cond, _ = face_dev(face)
        w = WH[face, pl.ds(8 * k, 8), :]
        for i in range(2):
            c = 2 * f + i
            v = jnp.where(cond, out[i] + w * BH[face, c, pl.ds(8 * k, 8), :], 0.0)
            carry = take(PP, on_face(compact, face, c, k), v, f, carry)
        return carry

    arrive_layer(1, 1, U)
    arrive_corners(1)
    for face in FACES:
        qmq = strip(1, U, face, finish_qh, qmq)
    told(6, 2)
    told(7, 8)

    group = lane // 16

    NALL = GX * GY
    xs = [lax.rem(gx + a, GX) for a in range(GX)]
    ys = [lax.rem(gy + a, GY) for a in range(GY)]

    def sum_copy(j):
        a, b = j // GY, j % GY
        slot = ((GX - a) % GX) * GY + (GY - b) % GY
        return pltpu.make_async_remote_copy(
            src_ref=A1R.at[pl.ds(0, 1), :], dst_ref=A1R.at[pl.ds(slot, 1), :],
            send_sem=a1s_sem, recv_sem=a1r_sem,
            device_id={"gx": xs[a], "gy": ys[b]}, device_id_type=MESH)

    def all_copies():
        rows = A1R.at[pl.ds(1, NALL - 1), :]
        return pltpu.make_async_remote_copy(
            src_ref=rows, dst_ref=rows, send_sem=a1s_sem, recv_sem=a1r_sem,
            device_id={"gx": xs[0], "gy": ys[1]}, device_id_type=MESH)

    def reduce_first(parts):
        mix = zero
        for i, v in enumerate(parts):
            for shift in (64, 32, 16):
                v = v + pltpu.roll(v, shift, 1)
            mix = jnp.where(group == i, v, mix)
        A1R[pl.ds(0, 1), :] = jnp.sum(mix, axis=0, keepdims=True)
        for j in range(1, NALL):
            sum_copy(j).start()

    def reduce_end():
        all_copies().wait_recv()
        v = jnp.broadcast_to(jnp.sum(A1R[...], axis=0, keepdims=True), (8, 128))
        for shift in (8, 4, 2, 1):
            v = v + pltpu.roll(v, 128 - shift, 1)
        return v

    def reduce_drain():
        all_copies().wait_send()

    def row(sums, i):
        return jnp.broadcast_to(sums[:, 16 * i:16 * i + 1], (8, 128))

    reduce_first((rr[0], rr[1], dq[0], dq[1], qq[0], qq[1], qmq[0], qmq[1]))
    for e, V in ((0, S), (1, U)):
        for l in range(2):
            drain_all([layer_copy(e, l, V, face) for face in FACES])
        drain_all([corner_copy(e, k) for k in range(4)])
    drain_all([model_copy(face) for face in FACES])
    drain_all([info_copy(face) for face in FACES])
    sums = reduce_end()

    cb, cq = [], []
    for f in range(2):
        norm0, curv0, qq0, qmq0 = (row(sums, 2 * i + f) for i in range(4))
        alpha0 = norm0 / curv0
        norm1 = norm0 - alpha0 * (2.0 * curv0 - alpha0 * qq0)
        beta = norm1 / norm0
        rq = curv0 - alpha0 * qq0
        rmr = curv0 - alpha0 * (2.0 * qq0 - alpha0 * qmq0)
        alpha1 = norm1 / (rmr + beta * (2.0 * rq + beta * curv0))
        cb.append(alpha0 + alpha1 * (1.0 + beta))
        cq.append(-(alpha0 * alpha1))

    GROWS = XL * YL // NGC
    def grad_copy(g):
        return pltpu.make_async_remote_copy(
            src_ref=GS.at[pl.ds(g * GROWS, GROWS), :], dst_ref=GR.at[pl.ds(g * GROWS, GROWS), :],
            send_sem=gs_sem.at[g], recv_sem=gr_sem.at[g], device_id={"af": 1 - af}, device_id_type=MESH)

    def outputs(i, _):
        for p in range(UN):
            r0 = pl.multiple_of(i * (UN * YL), 8) + p * YL
            for t in range(NT):
                r = r0 + t * 8
                g = zero
                for f in range(2):
                    fld, mis = [], []
                    for c in range(2):
                        n = 2 * f + c
                        v = cb[f] * B[n, pl.ds(r + YL, 8), :] + cq[f] * Q[n, pl.ds(r + YL, 8), :]
                        field_o[n, pl.ds(r, 8), :] = v
                        fld.append(v)
                        mis.append(cb[f] * U[n, pl.ds(r + YL, 8), :] + cq[f] * PP[n, pl.ds(r, 8), :]
                                   - S[n, pl.ds(r + YL, 8), :])
                    wr = -fld[0] - ATTENUATION * fld[1]
                    wi = ATTENUATION * fld[0] - fld[1]
                    g = g + sq[f] * (wr * mis[0] + wi * mis[1])
                GS[pl.ds(r, 8), :] = g
        return 0

    for g in range(NGC):
        lax.fori_loop(g * (XL // NGC // UN), (g + 1) * (XL // NGC // UN), outputs, 0)
        grad_copy(g).start()

    for g in range(NGC):
        grad_copy(g).wait_recv()

        def add(i, _):
            for n in range(8):
                o = pl.multiple_of(i * 64, 8) + n * 8
                grad_o[pl.ds(o, 8), :] = GS[pl.ds(o, 8), :] + GR[pl.ds(o, 8), :]
            return 0

        lax.fori_loop(g * GROWS // 64, (g + 1) * GROWS // 64, add, 0)

    for g in range(NGC):
        grad_copy(g).wait_send()
    reduce_drain()


def solution(mesh):
    GX, GY = mesh.shape["gx"], mesh.shape["gy"]

    def on_device(model, freq_sq, source, observed, receiver_depth):
        XL, YL, ZL = model.shape
        PX = XL + 2
        f32 = jnp.float32
        NGC = 4
        big = pltpu.VMEM((4, PX * YL, ZL), f32)
        col = pltpu.VMEM((XL * YL, ZL), f32)
        dma = pltpu.SemaphoreType.DMA
        field, grad = pl.pallas_call(
            functools.partial(kernel, (GX, GY, XL, YL, NGC)),
            out_shape=(jax.ShapeDtypeStruct((4, XL * YL, ZL), f32),
                       jax.ShapeDtypeStruct((XL * YL, ZL), f32)),
            in_specs=[pl.BlockSpec(memory_space=pltpu.HBM),
                      pl.BlockSpec(memory_space=pltpu.SMEM),
                      pl.BlockSpec(memory_space=pltpu.HBM),
                      pl.BlockSpec(memory_space=pltpu.HBM),
                      pl.BlockSpec(memory_space=pltpu.HBM)],
            out_specs=(pl.BlockSpec(memory_space=pltpu.VMEM),) * 2,
            scratch_shapes=[
                big, big, big, big,
                pltpu.VMEM((4, XL * YL, ZL), f32),
                col, col,
                pltpu.VMEM((4, XL * YL, ZL), f32),
                pltpu.VMEM((4 * XL, YL), f32),
                pltpu.VMEM((XL, YL), jnp.int32),
                pltpu.VMEM((2, 2, 4, YL + 16, ZL), f32),
                pltpu.VMEM((2, 2, 4, YL, ZL), f32),
                pltpu.VMEM((2, 2, 4, XL + 16, ZL), f32),
                pltpu.VMEM((2, 2, 4, XL, ZL), f32),
                pltpu.VMEM((2, 2, 2, 4, XL, ZL), f32),
                pltpu.VMEM((2, YL, ZL), f32),
                pltpu.VMEM((2, XL, ZL), f32),
                pltpu.VMEM((2, XL, ZL), f32),
                pltpu.VMEM((4, 8, ZL), f32),
                pltpu.VMEM((4, 8, ZL), f32),
                pltpu.VMEM((2, 4, 8, ZL), f32),
                pltpu.VMEM((2, 4, 8, ZL), f32),
                pltpu.VMEM((4, max(XL, YL), ZL), f32),
                pltpu.VMEM((4, 4, max(XL, YL), ZL), f32),
                pltpu.VMEM((4, 4, max(XL, YL), ZL), f32),
                pltpu.VMEM((GX * GY, ZL), f32),
                col, col,
                dma((7,)), dma((2, 2, 4)), dma((2, 2, 4)), dma((2, 4)), dma((2, 4)), dma((2, 4)), dma((2, 4)),
                dma(()), dma(()),
                pltpu.SemaphoreType.REGULAR((8, 4)),
                dma((NGC,)), dma((NGC,)),
            ],
            compiler_params=pltpu.CompilerParams(
                collective_id=0, has_side_effects=True, vmem_limit_bytes=26 * 2**20),
        )(*[pltpu.with_memory_space_constraint(a, pltpu.HBM) for a in (
            model.reshape(XL * YL, ZL), freq_sq, source.reshape(4, XL * YL, ZL),
            observed.reshape(4 * XL, YL), receiver_depth)])
        return field.reshape(2, 2, XL, YL, ZL), grad.reshape(XL, YL, ZL)

    in_specs = (
        P("gx", "gy", None),
        P("af"),
        P("af", None, "gx", "gy", None),
        P("af", None, "gx", "gy"),
        P("gx", "gy"),
    )
    out_specs = (P("af", None, "gx", "gy", None), P("gx", "gy", None))
    return jax.shard_map(
        on_device, mesh=mesh, in_specs=in_specs, out_specs=out_specs, check_vma=False
    )
```

```python
import functools

import jax
import jax.numpy as jnp
from jax import lax
from jax.experimental import pallas as pl
from jax.experimental.pallas import tpu as pltpu
from jax.sharding import PartitionSpec as P

MESH = pl.DeviceIdType.MESH
ATTENUATION = 0.2
PENALTY = 4.0


def kernel(dims, model_h, fsq, src_h, obs_h, depth_h, field_o, grad_o,
           S, B, U, Q, PP, M, W, WO, OB, DP, X1, X2, Y1, Y2, YS, MX, MY, MYS, IS, IR, CS, CR, WH, WOH, BH,
           A1R, GS, GR,
           load_sem, hs_sem, hr_sem, ms_sem, mr_sem, cs_sem, cr_sem,
           a1s_sem, a1r_sem, tok_sem, gs_sem, gr_sem):
    GX, GY, XL, YL, NGC = dims
    PX = XL + 2
    NT = YL // 8
    XT = XL // 8
    gx = lax.axis_index("gx")
    gy = lax.axis_index("gy")
    af = lax.axis_index("af")

    def axis_peer(n, sign, axis):
        at, size, name = ((gx, GX, "gx"), (gy, GY, "gy"))[axis]
        return (at >= n, {name: at - n}) if sign < 0 else (at < size - n, {name: at + n})

    barrier = pltpu.get_barrier_semaphore()
    pl.semaphore_signal(barrier, inc=1, device_id={"af": 1 - af}, device_id_type=MESH)
    peers = jnp.int32(1)
    for axis in range(2):
        for sign in (-1, 1):
            cond, dev = axis_peer(1, sign, axis)
            peers = peers + cond.astype(jnp.int32)

            @pl.when(cond)
            def _():
                pl.semaphore_signal(barrier, inc=1, device_id=dev, device_id_type=MESH)

    def tell(r, n):
        for axis in range(2):
            for sign in (-1, 1):
                cond, dev = axis_peer(n, sign, axis)

                @pl.when(cond)
                def _():
                    pl.semaphore_signal(tok_sem.at[r, 2 * axis + (sign < 0)], inc=1, device_id=dev,
                                        device_id_type=MESH)

    def told(r, n):
        for axis in range(2):
            for sign in (-1, 1):
                cond, dev = axis_peer(n, sign, axis)

                @pl.when(cond)
                def _():
                    pl.semaphore_wait(tok_sem.at[r, 2 * axis + (sign > 0)], 1)

    loads = [
        pltpu.make_async_copy(depth_h, DP, load_sem.at[4]),
        pltpu.make_async_copy(obs_h, OB, load_sem.at[5]),
        pltpu.make_async_copy(model_h, M, load_sem.at[6]),
    ] + [
        pltpu.make_async_copy(src_h.at[c], S.at[c, pl.ds(YL, XL * YL), :], load_sem.at[c]) for c in range(4)
    ]
    for cp in loads:
        cp.start()

    zero = jnp.zeros((8, 128), jnp.float32)

    for ref in (S, B, U, Q):
        for c in range(4):
            for xx in (0, PX - 1):
                for t in range(NT):
                    ref[c, pl.ds(xx * YL + t * 8, 8), :] = zero

    def clear(ref, side, count):
        for e in range(2):
            for c in range(4):
                for r in range(0, count, 8):
                    ref[e, side, c, pl.ds(8 + r, 8), :] = zero

    has = ((gx > 0, gx < GX - 1), (gy > 0, gy < GY - 1))
    for side in range(2):
        pl.when(jnp.logical_not(has[0][side]))(functools.partial(clear, X1, side, YL))
        pl.when(jnp.logical_not(has[1][side]))(functools.partial(clear, Y1, side, XL))
    for sx in range(2):
        for sy in range(2):
            @pl.when(jnp.logical_not(jnp.logical_and(has[0][sx], has[1][sy])))
            def _():
                for e in range(2):
                    CR[e, 2 * sx + sy] = zero

    for face in range(4):
        @pl.when(jnp.logical_not(has[face // 2][face % 2]))
        def _():
            IR[face] = zero

    def remote(src, dst, ssem, rsem, dev):
        return pltpu.make_async_remote_copy(
            src_ref=src, dst_ref=dst, send_sem=ssem, recv_sem=rsem, device_id=dev, device_id_type=MESH)

    def face_dev(face):
        axis, side = face // 2, face % 2
        step = 2 * side - 1
        return has[axis][side], ({"gx": gx + step} if axis == 0 else {"gy": gy + step})

    def layer_copy(e, l, V, face):
        axis, side = face // 2, face % 2
        there = 1 - side
        if axis == 0:
            plane = l if side == 0 else XL - 1 - l
            src = V.at[:, pl.ds((1 + plane) * YL, YL), :]
            dst = X1.at[e, there, :, pl.ds(8, YL), :] if l == 0 else X2.at[e, there]
        else:
            src = YS.at[e, side, l]
            dst = Y1.at[e, there, :, pl.ds(8, XL), :] if l == 0 else Y2.at[e, there]
        cond, dev = face_dev(face)
        return cond, remote(src, dst, hs_sem.at[e, l, face], hr_sem.at[e, l, 2 * axis + there], dev)

    def model_copy(face):
        axis, side = face // 2, face % 2
        there = 1 - side
        if axis == 0:
            src, dst = M.at[pl.ds(side * (XL - 1) * YL, YL), :], MX.at[there]
        else:
            src, dst = MYS.at[side], MY.at[there]
        cond, dev = face_dev(face)
        return cond, remote(src, dst, ms_sem.at[0, face], mr_sem.at[0, 2 * axis + there], dev)

    def info_copy(face):
        axis, side = face // 2, face % 2
        there = 2 * axis + 1 - side
        cond, dev = face_dev(face)
        return cond, remote(IS.at[face], IR.at[there], ms_sem.at[1, face], mr_sem.at[1, there], dev)

    def corner_copy(e, k):
        sx, sy = k // 2, k % 2
        return jnp.logical_and(has[0][sx], has[1][sy]), remote(
            CS.at[e, k, pl.ds(0, 4), :], CR.at[e, 3 - k, pl.ds(0, 4), :], cs_sem.at[e, k], cr_sem.at[e, 3 - k],
            {"gx": gx + (2 * sx - 1), "gy": gy + (2 * sy - 1)})

    FACES = (0, 1, 2, 3)
    other = lambda face: face ^ 1

    def start_all(copies):
        for cond, cp in copies:
            pl.when(cond)(cp.start)

    def drain_all(copies):
        for cond, cp in copies:
            pl.when(cond)(cp.wait_send)

    def arrive_all(make, faces):
        for face in faces:
            cond, _ = face_dev(face)
            pl.when(cond)(make(other(face))[1].wait_recv)

    def arrive_layer(e, l, V):
        arrive_all(lambda face: layer_copy(e, l, V, face), FACES)

    def arrive_corners(e):
        for k in range(4):
            pl.when(jnp.logical_and(has[0][k // 2], has[1][k % 2]))(corner_copy(e, 3 - k)[1].wait_recv)
        for k in range(4):
            sx, sy = k // 2, k % 2
            for c in range(4):
                v = CR[e, k, pl.ds(c, 1), :]
                X1[e, sx, c, pl.ds(8 + YL if sy else 7, 1), :] = v
                Y1[e, sy, c, pl.ds(8 + XL if sx else 7, 1), :] = v

    def pack_layer(e, l, V):
        for side in range(2):
            y = l if side == 0 else YL - 1 - l
            for c in range(4):
                for k in range(XT):
                    YS[e, side, l, c, pl.ds(k * 8, 8), :] = V[c, pl.ds((1 + 8 * k) * YL + y, 8, stride=YL), :]

    def pack_corners(e, V):
        for k in range(4):
            o = (1 + (XL - 1) * (k // 2)) * YL + (YL - 1) * (k % 2)
            for c in range(4):
                CS[e, k, pl.ds(c, 1), :] = V[c, pl.ds(o, 1), :]

    lane = lax.broadcasted_iota(jnp.int32, (8, 128), 1)
    at_first = lane == 0
    at_last = lane == 127
    sq = [fsq[0], fsq[1]]

    sub = lax.broadcasted_iota(jnp.int32, (8, 128), 0)
    UN = 2

    def around(V, c, o, t):
        cen = V[c, pl.ds(o, 8), :]
        total = V[c, pl.ds(o - YL, 8), :] + V[c, pl.ds(o + YL, 8), :]
        ym, yp = V[c, pl.ds(o - 1, 8), :], V[c, pl.ds(o + 1, 8), :]
        if t == 0:
            ym = jnp.where(sub == 0, 0.0, ym)
        if t == NT - 1:
            yp = jnp.where(sub == 7, 0.0, yp)
        total = total + (ym + yp)
        lo = jnp.where(at_first, 0.0, pltpu.roll(cen, 1, 1))
        hi = jnp.where(at_last, 0.0, pltpu.roll(cen, 127, 1))
        return cen, total + (lo + hi)

    def coefs(f, m, sign):
        k = sq[f] * m
        return 6.0 - k, (sign * ATTENUATION) * k

    def tiles_of(V, sign, finish, r0, tiles, carry):
        for t in tiles:
            m = M[pl.ds(r0 + t * 8, 8), :]
            for f in range(2):
                cr, ci = coefs(f, m, sign)
                o = r0 + YL + t * 8
                re, nre = around(V, 2 * f, o, t)
                im, nim = around(V, 2 * f + 1, o, t)
                out = (cr * re - ci * im - nre, cr * im + ci * re - nim)
                carry = finish(f, o, r0 + t * 8, (re, im), out, carry)
        return carry

    def planes(V, sign, finish, carry, lo, hi, un, tiles):
        def body(i, carry):
            for p in range(un):
                r0 = pl.multiple_of(i * (un * YL), 8) + (lo + p) * YL
                carry = tiles_of(V, sign, finish, r0, tiles, carry)
            return carry
        if not tiles:
            return carry
        return lax.fori_loop(0, (hi - lo) // un, body, carry)

    def sweep(V, sign, finish, carry):
        return planes(V, sign, finish, carry, 0, XL, UN, range(NT))

    def sweep_inner(V, sign, finish, carry):
        return planes(V, sign, finish, carry, 2, XL - 2, 4, range(1, NT - 1))

    def sweep_outer(V, sign, finish, carry):
        carry = planes(V, sign, finish, carry, 2, XL - 2, 4, (0, NT - 1))
        def ends(i, carry):
            for p in range(2):
                r0 = pl.multiple_of(i * ((XL - 2) * YL), 8) + p * YL
                carry = tiles_of(V, sign, finish, r0, range(NT), carry)
            return carry
        return lax.fori_loop(0, 2, ends, carry)

    def strip(e, V, face, finish, carry):
        axis, side = face // 2, face % 2
        H1, H2, MH, L = (X1, X2, MX, YL) if axis == 0 else (Y1, Y2, MY, XL)
        for k in range(L // 8):
            m = MH[side, pl.ds(8 * k, 8), :]
            for f in range(2):
                cr, ci = coefs(f, m, -1.0)
                cen, nb = [], []
                for c in (2 * f, 2 * f + 1):
                    v = H1[e, side, c, pl.ds(8 + 8 * k, 8), :]
                    if axis == 0:
                        inward = V[c, pl.ds((1 + side * (XL - 1)) * YL + 8 * k, 8), :]
                    else:
                        inward = V[c, pl.ds((1 + 8 * k) * YL + side * (YL - 1), 8, stride=YL), :]
                    total = (H2[e, side, c, pl.ds(8 * k, 8), :] + inward) + (
                        H1[e, side, c, pl.ds(7 + 8 * k, 8), :] + H1[e, side, c, pl.ds(9 + 8 * k, 8), :])
                    lo = jnp.where(at_first, 0.0, pltpu.roll(v, 1, 1))
                    hi = jnp.where(at_last, 0.0, pltpu.roll(v, 127, 1))
                    cen.append(v)
                    nb.append(total + (lo + hi))
                out = (cr * cen[0] - ci * cen[1] - nb[0], cr * cen[1] + ci * cen[0] - nb[1])
                carry = finish(face, k, f, out, carry)
        return carry

    def on_face(rows, face, c, k):
        axis, side = face // 2, face % 2
        if axis == 0:
            return rows(c, 1 + side * (XL - 1), 8 * k, False)
        return rows(c, 1 + 8 * k, side * (YL - 1), True)

    def take(ref, idx, h, f, carry):
        old = ref[idx[0], idx[1], :]
        ref[idx[0], idx[1], :] = old - h
        d = h * (h - 2.0 * old)
        return tuple(carry[i] + d if i == f else carry[i] for i in range(2))

    def correct(e, ref, carry):
        for face in range(4):
            H1, L = (X1, YL) if face < 2 else (Y1, XL)
            for c in range(4):
                for k in range(L // 8):
                    h = H1[e, face % 2, c, pl.ds(8 + 8 * k, 8), :]
                    carry = take(ref, on_face(padded, face, c, k), h, c // 2, carry)
        return carry

    def padded(c, xx, yy, strided):
        o = xx * YL + yy
        return c, pl.ds(o, 8, stride=YL) if strided else pl.ds(o, 8)

    def compact(c, xx, yy, strided):
        return padded(c, xx - 1, yy, strided)

    for cp in loads[3:]:
        cp.wait()
    pl.semaphore_wait(barrier, peers)
    start_all([layer_copy(0, l, S, face) for l in range(2) for face in (0, 1)])
    tell(0, 1)
    for l in range(2):
        pack_layer(0, l, S)
        start_all([layer_copy(0, l, S, face) for face in (2, 3)])
    pack_corners(0, S)
    loads[0].wait()
    loads[1].wait()
    dt = jnp.transpose(jnp.concatenate(
        [DP[...].astype(jnp.float32), jnp.zeros((XL, 128 - YL), jnp.float32)], axis=1))
    ot = jnp.transpose(jnp.concatenate(
        [OB[...], jnp.zeros((4 * XL, 128 - YL), jnp.float32)], axis=1))
    for face in range(4):
        IS[face] = zero
    for side in range(2):
        x, y = side * (XL - 1), side * (YL - 1)
        for c in range(4):
            IS[side, c:c + 1, 0:YL] = OB[c * XL + x:c * XL + x + 1, :]
        IS[side, 4:5, 0:YL] = DP[x:x + 1, :].astype(jnp.float32)
        IS[2 + side, 0:1, 0:4 * XL] = ot[y:y + 1, :]
        IS[2 + side, 1:2, 0:XL] = dt[y:y + 1, :]
    loads[2].wait()
    for side in range(2):
        for k in range(XT):
            MYS[side, pl.ds(8 * k, 8), :] = M[pl.ds(8 * k * YL + side * (YL - 1), 8, stride=YL), :]
    start_all([info_copy(face) for face in FACES])
    start_all([model_copy(face) for face in FACES])

    lanef = lane.astype(jnp.float32)
    for x in range(XL):
        for t in range(NT):
            d = jnp.broadcast_to(dt[t * 8:t * 8 + 8, x:x + 1], (8, 128))
            w = jnp.where(lanef == d, PENALTY, 0.0)
            W[pl.ds(x * YL + t * 8, 8), :] = w
            for c in range(4):
                ob = jnp.broadcast_to(ot[t * 8:t * 8 + 8, c * XL + x:c * XL + x + 1], (8, 128))
                WO[c, pl.ds(x * YL + t * 8, 8), :] = w * ob

    def finish_b(f, o, r, cen, out, carry):
        acc = carry[f]
        for c in range(2):
            v = out[c] + WO[2 * f + c, pl.ds(r, 8), :]
            B[2 * f + c, pl.ds(o, 8), :] = v
            acc = acc + v * v
        return tuple(acc if i == f else carry[i] for i in range(2))

    told(0, 1)
    start_all([corner_copy(0, k) for k in range(4)])
    tell(1, 2)
    rr = sweep(S, -1.0, finish_b, (zero, zero))
    told(1, 2)
    tell(2, 4)

    def finish_u(f, o, r, cen, out, carry):
        acc = carry[f]
        for c in range(2):
            U[2 * f + c, pl.ds(o, 8), :] = out[c]
            acc = acc + out[c] * out[c]
        return tuple(acc if i == f else carry[i] for i in range(2))

    dq = sweep_inner(B, 1.0, finish_u, (zero, zero))
    arrive_layer(0, 0, S)
    rr = correct(0, B, rr)
    told(2, 4)
    tell(3, 8)
    dq = sweep_outer(B, 1.0, finish_u, dq)

    arrive_all(info_copy, FACES)
    it = jnp.transpose(jnp.concatenate(
        [IR[face] for face in range(4)] + [jnp.zeros((96, 128), jnp.float32)], axis=0))
    for face in range(4):
        L = YL if face < 2 else XL
        for k in range(L // 8):
            if face < 2:
                d = it[8 * k:8 * k + 8, 8 * face + 4:8 * face + 5]
                obs = [it[8 * k:8 * k + 8, 8 * face + c:8 * face + c + 1] for c in range(4)]
            else:
                d = it[8 * k:8 * k + 8, 8 * face + 1:8 * face + 2]
                obs = [it[c * XL + 8 * k:c * XL + 8 * k + 8, 8 * face:8 * face + 1] for c in range(4)]
            w = jnp.where(lanef == jnp.broadcast_to(d, (8, 128)), PENALTY, 0.0)
            WH[face, pl.ds(8 * k, 8), :] = w
            for c in range(4):
                WOH[face, c, pl.ds(8 * k, 8), :] = w * jnp.broadcast_to(obs[c], (8, 128))

    def finish_bh(face, k, f, out, carry):
        cond, _ = face_dev(face)
        for i in range(2):
            c = 2 * f + i
            v = jnp.where(cond, out[i] + WOH[face, c, pl.ds(8 * k, 8), :], 0.0)
            BH[face, c, pl.ds(8 * k, 8), :] = v
            carry = take(U, on_face(padded, face, c, k), v, f, carry)
        return carry

    arrive_all(model_copy, FACES)
    arrive_layer(0, 1, S)
    arrive_corners(0)
    for face in FACES:
        dq = strip(0, S, face, finish_bh, dq)
    pack_corners(1, U)
    start_all([corner_copy(1, k) for k in range(4)])
    start_all([layer_copy(1, l, U, face) for l in range(2) for face in (0, 1)])
    for l in range(2):
        pack_layer(1, l, U)
        start_all([layer_copy(1, l, U, face) for face in (2, 3)])
    told(3, 8)
    tell(4, 1)
    tell(5, 4)

    def finish_q(f, o, r, cen, out, carry):
        dq, qq = carry[f], carry[2 + f]
        w = W[pl.ds(r, 8), :]
        for c in range(2):
            b = B[2 * f + c, pl.ds(o, 8), :]
            wb = w * b
            v = out[c] + wb
            Q[2 * f + c, pl.ds(o, 8), :] = v
            dq = dq + wb * b
            qq = qq + v * v
        carry = list(carry)
        carry[f], carry[2 + f] = dq, qq
        return tuple(carry)

    carry = sweep(U, -1.0, finish_q, tuple(dq) + (zero, zero))
    dq, qq = carry[:2], carry[2:]
    def finish_p(f, o, r, cen, out, carry):
        acc = carry[f]
        w = W[pl.ds(r, 8), :]
        for c in range(2):
            PP[2 * f + c, pl.ds(r, 8), :] = out[c]
            acc = acc + (out[c] * out[c] + w * (cen[c] * cen[c]))
        return tuple(acc if i == f else carry[i] for i in range(2))

    told(4, 1)
    told(5, 4)
    tell(6, 2)
    tell(7, 8)
    qmq = sweep_inner(Q, 1.0, finish_p, (zero, zero))
    arrive_layer(1, 0, U)
    qq = correct(1, Q, qq)
    qmq = sweep_outer(Q, 1.0, finish_p, qmq)

    def finish_qh(face, k, f, out, carry):
        cond, _ = face_dev(face)
        w = WH[face, pl.ds(8 * k, 8), :]
        for i in range(2):
            c = 2 * f + i
            v = jnp.where(cond, out[i] + w * BH[face, c, pl.ds(8 * k, 8), :], 0.0)
            carry = take(PP, on_face(compact, face, c, k), v, f, carry)
        return carry

    arrive_layer(1, 1, U)
    arrive_corners(1)
    for face in FACES:
        qmq = strip(1, U, face, finish_qh, qmq)
    told(6, 2)
    told(7, 8)

    group = lane // 16

    NALL = GX * GY
    xs = [lax.rem(gx + a, GX) for a in range(GX)]
    ys = [lax.rem(gy + a, GY) for a in range(GY)]

    def sum_copy(j):
        a, b = j // GY, j % GY
        slot = ((GX - a) % GX) * GY + (GY - b) % GY
        return pltpu.make_async_remote_copy(
            src_ref=A1R.at[pl.ds(0, 1), :], dst_ref=A1R.at[pl.ds(slot, 1), :],
            send_sem=a1s_sem, recv_sem=a1r_sem,
            device_id={"gx": xs[a], "gy": ys[b]}, device_id_type=MESH)

    def all_copies():
        rows = A1R.at[pl.ds(1, NALL - 1), :]
        return pltpu.make_async_remote_copy(
            src_ref=rows, dst_ref=rows, send_sem=a1s_sem, recv_sem=a1r_sem,
            device_id={"gx": xs[0], "gy": ys[1]}, device_id_type=MESH)

    def reduce_first(parts):
        mix = zero
        for i, v in enumerate(parts):
            for shift in (64, 32, 16):
                v = v + pltpu.roll(v, shift, 1)
            mix = jnp.where(group == i, v, mix)
        A1R[pl.ds(0, 1), :] = jnp.sum(mix, axis=0, keepdims=True)
        for j in range(1, NALL):
            sum_copy(j).start()

    def reduce_end():
        all_copies().wait_recv()
        v = jnp.broadcast_to(jnp.sum(A1R[...], axis=0, keepdims=True), (8, 128))
        for shift in (8, 4, 2, 1):
            v = v + pltpu.roll(v, 128 - shift, 1)
        return v

    def reduce_drain():
        all_copies().wait_send()

    def row(sums, i):
        return jnp.broadcast_to(sums[:, 16 * i:16 * i + 1], (8, 128))

    reduce_first((rr[0], rr[1], dq[0], dq[1], qq[0], qq[1], qmq[0], qmq[1]))
    for e, V in ((0, S), (1, U)):
        for l in range(2):
            drain_all([layer_copy(e, l, V, face) for face in FACES])
        drain_all([corner_copy(e, k) for k in range(4)])
    drain_all([model_copy(face) for face in FACES])
    drain_all([info_copy(face) for face in FACES])
    sums = reduce_end()

    cb, cq = [], []
    for f in range(2):
        norm0, curv0, qq0, qmq0 = (row(sums, 2 * i + f) for i in range(4))
        alpha0 = norm0 / curv0
        norm1 = norm0 - alpha0 * (2.0 * curv0 - alpha0 * qq0)
        beta = norm1 / norm0
        rq = curv0 - alpha0 * qq0
        rmr = curv0 - alpha0 * (2.0 * qq0 - alpha0 * qmq0)
        alpha1 = norm1 / (rmr + beta * (2.0 * rq + beta * curv0))
        cb.append(alpha0 + alpha1 * (1.0 + beta))
        cq.append(-(alpha0 * alpha1))

    GROWS = XL * YL // NGC
    def grad_copy(g):
        return pltpu.make_async_remote_copy(
            src_ref=GS.at[pl.ds(g * GROWS, GROWS), :], dst_ref=GR.at[pl.ds(g * GROWS, GROWS), :],
            send_sem=gs_sem.at[g], recv_sem=gr_sem.at[g], device_id={"af": 1 - af}, device_id_type=MESH)

    OUN = 4

    def outputs(i, _):
        for p in range(OUN):
            r0 = pl.multiple_of(i * (OUN * YL), 8) + p * YL
            for t in range(NT):
                r = r0 + t * 8
                g = zero
                for f in range(2):
                    fld, mis = [], []
                    for c in range(2):
                        n = 2 * f + c
                        v = cb[f] * B[n, pl.ds(r + YL, 8), :] + cq[f] * Q[n, pl.ds(r + YL, 8), :]
                        field_o[n, pl.ds(r, 8), :] = v
                        fld.append(v)
                        mis.append(cb[f] * U[n, pl.ds(r + YL, 8), :] + cq[f] * PP[n, pl.ds(r, 8), :]
                                   - S[n, pl.ds(r + YL, 8), :])
                    wr = -fld[0] - ATTENUATION * fld[1]
                    wi = ATTENUATION * fld[0] - fld[1]
                    g = g + sq[f] * (wr * mis[0] + wi * mis[1])
                GS[pl.ds(r, 8), :] = g
        return 0

    for g in range(NGC):
        lax.fori_loop(g * (XL // NGC // OUN), (g + 1) * (XL // NGC // OUN), outputs, 0)
        grad_copy(g).start()

    for g in range(NGC):
        grad_copy(g).wait_recv()

        def add(i, _):
            for n in range(8):
                o = pl.multiple_of(i * 64, 8) + n * 8
                grad_o[pl.ds(o, 8), :] = GS[pl.ds(o, 8), :] + GR[pl.ds(o, 8), :]
            return 0

        lax.fori_loop(g * GROWS // 64, (g + 1) * GROWS // 64, add, 0)

    for g in range(NGC):
        grad_copy(g).wait_send()
    reduce_drain()


def solution(mesh):
    GX, GY = mesh.shape["gx"], mesh.shape["gy"]

    def on_device(model, freq_sq, source, observed, receiver_depth):
        XL, YL, ZL = model.shape
        PX = XL + 2
        f32 = jnp.float32
        NGC = 4
        big = pltpu.VMEM((4, PX * YL, ZL), f32)
        col = pltpu.VMEM((XL * YL, ZL), f32)
        dma = pltpu.SemaphoreType.DMA
        field, grad = pl.pallas_call(
            functools.partial(kernel, (GX, GY, XL, YL, NGC)),
            out_shape=(jax.ShapeDtypeStruct((4, XL * YL, ZL), f32),
                       jax.ShapeDtypeStruct((XL * YL, ZL), f32)),
            in_specs=[pl.BlockSpec(memory_space=pltpu.HBM),
                      pl.BlockSpec(memory_space=pltpu.SMEM),
                      pl.BlockSpec(memory_space=pltpu.HBM),
                      pl.BlockSpec(memory_space=pltpu.HBM),
                      pl.BlockSpec(memory_space=pltpu.HBM)],
            out_specs=(pl.BlockSpec(memory_space=pltpu.VMEM),) * 2,
            scratch_shapes=[
                big, big, big, big,
                pltpu.VMEM((4, XL * YL, ZL), f32),
                col, col,
                pltpu.VMEM((4, XL * YL, ZL), f32),
                pltpu.VMEM((4 * XL, YL), f32),
                pltpu.VMEM((XL, YL), jnp.int32),
                pltpu.VMEM((2, 2, 4, YL + 16, ZL), f32),
                pltpu.VMEM((2, 2, 4, YL, ZL), f32),
                pltpu.VMEM((2, 2, 4, XL + 16, ZL), f32),
                pltpu.VMEM((2, 2, 4, XL, ZL), f32),
                pltpu.VMEM((2, 2, 2, 4, XL, ZL), f32),
                pltpu.VMEM((2, YL, ZL), f32),
                pltpu.VMEM((2, XL, ZL), f32),
                pltpu.VMEM((2, XL, ZL), f32),
                pltpu.VMEM((4, 8, ZL), f32),
                pltpu.VMEM((4, 8, ZL), f32),
                pltpu.VMEM((2, 4, 8, ZL), f32),
                pltpu.VMEM((2, 4, 8, ZL), f32),
                pltpu.VMEM((4, max(XL, YL), ZL), f32),
                pltpu.VMEM((4, 4, max(XL, YL), ZL), f32),
                pltpu.VMEM((4, 4, max(XL, YL), ZL), f32),
                pltpu.VMEM((GX * GY, ZL), f32),
                col, col,
                dma((7,)), dma((2, 2, 4)), dma((2, 2, 4)), dma((2, 4)), dma((2, 4)), dma((2, 4)), dma((2, 4)),
                dma(()), dma(()),
                pltpu.SemaphoreType.REGULAR((8, 4)),
                dma((NGC,)), dma((NGC,)),
            ],
            compiler_params=pltpu.CompilerParams(
                collective_id=0, has_side_effects=True, vmem_limit_bytes=26 * 2**20),
        )(*[pltpu.with_memory_space_constraint(a, pltpu.HBM) for a in (
            model.reshape(XL * YL, ZL), freq_sq, source.reshape(4, XL * YL, ZL),
            observed.reshape(4 * XL, YL), receiver_depth)])
        return field.reshape(2, 2, XL, YL, ZL), grad.reshape(XL, YL, ZL)

    in_specs = (
        P("gx", "gy", None),
        P("af"),
        P("af", None, "gx", "gy", None),
        P("af", None, "gx", "gy"),
        P("gx", "gy"),
    )
    out_specs = (P("af", None, "gx", "gy", None), P("gx", "gy", None))
    return jax.shard_map(
        on_device, mesh=mesh, in_specs=in_specs, out_specs=out_specs, check_vma=False
    )
```
